32 devices in a mesh: sec: 2 (over core), var: 4 (over z), trait: 4 (over y, x).
Axes of the slice: x: 2, y: 2, z: 4, core: 2. Of those that a mesh axis runs over, the one named last changes fastest.
Arguments:
- z_typed: bfloat16 [32768, 512], P(('sec', 'var'), 'trait'), may hold values from -6 to 6
- band_inverse: bfloat16 [256, 128, 384], P(('sec', 'var')), may hold values from -0.3125 to 0.3125
- ld_untyped: bfloat16 [512, 128, 512], P(('sec', 'var')), may hold values from -0.375 to 0.375
- trait_mix: bfloat16 [512, 512], replicated, may hold values from -0.25 to 0.25
- win_start: int32 [512], P(('sec', 'var')), may hold values from 0 to 255, as said below
- win_count: int32 [512], P(('sec', 'var')), may hold values from 1 to 4, as said below
Outputs:
- imputed_mixed: bfloat16 [65536, 512], P(('sec', 'var'), 'trait')
The draws below stay inside these ranges and needn't reach their ends.
Inputs may be any that keep to these rules, and one draw needn't show every extreme that they name: Windows follow chromosome order: within the 64 untyped blocks of one index g of sec+var, win_start never falls, and every window lies in typed blocks g * 32 - 32 to (g + 1) * 32 + 31; the first window of each index starts at its lower end (or at 0) and the last one ends at its upper end (or at the chromosome's end). win_start + win_count never exceeds 256.
All inputs are finite; a program needn't handle non-finite values.
Results may differ from the reference program's by a relative error of at most 0.0057.
Values may be sent and summed in bfloat16 or wider, within the bound.
A program may use at most 64 MiB of HBM per device.

```python
import jax
import jax.numpy as jnp
from jax import lax

BLK = 128
WIN = 4
TRAITS = 512
TB_DEV = 32
UB_DEV = 64
REACH = 32
VGROUPS = 8
TYPED_BLOCKS = 256
TYPED_ROWS = 32768
UNTYPED_BLOCKS = 512


def window_plan(key):
    subkeys = jax.random.split(jax.random.fold_in(key, 7), VGROUPS)
    owners = jnp.arange(VGROUPS, dtype=jnp.int32)
    span = TB_DEV + 2 * REACH - WIN

    def one_owner(owner_key, owner):
        first_key, second_key = jax.random.split(owner_key, 2)
        lowest = owner * TB_DEV - REACH
        offsets = jnp.sort(jax.random.randint(first_key, (UB_DEV,), 0, span + 1))
        offsets = offsets.at[0].set(0).at[UB_DEV - 1].set(span)
        counts = jax.random.randint(second_key, (UB_DEV,), 1, WIN + 1)
        counts = counts.at[0].set(WIN).at[UB_DEV - 1].set(WIN)
        starts = jnp.clip(lowest + offsets, 0, TYPED_BLOCKS - 1)
        counts = jnp.minimum(counts, TYPED_BLOCKS - starts)
        return (starts, counts)
    starts, counts = jax.vmap(one_owner)(subkeys, owners)
    return (starts.reshape(-1).astype(jnp.int32), counts.reshape(-1).astype(jnp.int32))


def draw_win_start(key, part):
    return window_plan(key)[0]


def draw_win_count(key, part):
    return window_plan(key)[1]


def block_levels(own_key, extent, cuts, low, top_value):
    loudness = 1.0
    for axis_at, blocks in cuts:
        heights = jax.random.uniform(jax.random.fold_in(jax.random.fold_in(own_key, 6), axis_at), (blocks,), jnp.float32, low / len(cuts), top_value / len(cuts))
        loudness = loudness * jnp.repeat(jnp.exp(heights), extent[axis_at] // blocks).reshape((-1,) + (1,) * (len(extent) - 1 - axis_at))
    return loudness


def gaussian(key, shape, deviation, limit, shards=(), kind=jnp.bfloat16):
    values = jax.random.normal(key, shape, jnp.float32) * deviation
    if len(shards) > 0:
        values = block_levels(key, shape, shards, -0.22, 0.18) * values
    return jnp.clip(values, min=-limit, max=limit).astype(kind)


def setup_inputs(seed: int = 0) -> dict:
    streams_of = jax.random.split(jax.random.key(seed), 7)
    return {
        "z_typed": gaussian(streams_of[0], (TYPED_ROWS, TRAITS), 1.0, 6.0, ((0, 8), (1, 4))),
        "band_inverse": gaussian(streams_of[1], (TYPED_BLOCKS, BLK, 3 * BLK), (3 * BLK) ** -0.5, 0.3125, ((0, 8),)),
        "ld_untyped": gaussian(streams_of[2], (UNTYPED_BLOCKS, BLK, WIN * BLK), (2 * BLK) ** -0.5, 0.375, ((0, 8),)),
        "trait_mix": gaussian(streams_of[3], (TRAITS, TRAITS), TRAITS ** -0.5, 0.25),
        "win_start": draw_win_start(jax.random.fold_in(streams_of[6], 71), 0),
        "win_count": draw_win_count(jax.random.fold_in(streams_of[6], 71), 0),
    }


def whiten(z_typed, band_inverse):
    blocks = z_typed.shape[0] // BLK
    padded = jnp.pad(z_typed, ((BLK, BLK), (0, 0)))
    stacked = jnp.concatenate([padded[k * BLK:(k + blocks) * BLK].reshape(blocks, BLK, z_typed.shape[1]) for k in range(3)], axis=1)
    return jnp.einsum("bij,bjc->bic", band_inverse.astype(jnp.float32), stacked.astype(jnp.float32)).astype(jnp.bfloat16)


def reference(z_typed, band_inverse, ld_untyped, trait_mix, win_start, win_count):
    whitened = whiten(z_typed, band_inverse)
    mixed = jnp.dot(whitened.reshape(TYPED_ROWS, TRAITS), trait_mix, preferred_element_type=jnp.float32).astype(jnp.bfloat16)
    mixed = mixed.reshape(TYPED_BLOCKS, BLK, TRAITS)
    window_steps = jnp.arange(WIN, dtype=jnp.int32)

    def impute(inputs):
        ld_group, starts, counts = inputs
        wanted = (starts[:, None] + window_steps[None, :]).astype(jnp.int32)
        usable = window_steps[None, :] < counts[:, None]
        picked = mixed[jnp.clip(wanted, 0, TYPED_BLOCKS - 1)]
        picked = jnp.where(usable[:, :, None, None], picked, jnp.zeros_like(picked))
        picked = picked.reshape(picked.shape[0], WIN * BLK, TRAITS)
        return jnp.einsum("uij,ujc->uic", ld_group.astype(jnp.float32), picked.astype(jnp.float32)).astype(jnp.bfloat16)

    grouped = (ld_untyped.reshape(VGROUPS, UB_DEV, BLK, WIN * BLK), win_start.reshape(VGROUPS, UB_DEV), win_count.reshape(VGROUPS, UB_DEV))
    imputed = lax.map(impute, grouped)
    return imputed.reshape(UNTYPED_BLOCKS * BLK, TRAITS)
```

```python
import functools

import jax
import jax.numpy as jnp
from jax import lax
from jax.experimental import pallas as pl
from jax.experimental.pallas import tpu as pltpu
from jax.sharding import PartitionSpec as P

BLK = 128
WIN = 4
LATE = 4
SHIFT = LATE - 1
FIRST = 4
CHUNK = 4
AHEAD = 2
LAG = 1
BY_PARTS = 1
FOREIGN_AT = 5
GROUP = 8
MESH = pl.DeviceIdType.MESH


def chunk_plan(blocks):
    first = blocks // 2 - FIRST // 2
    starts = []
    at = LATE
    while at < blocks - LATE:
        if at == first:
            at += FIRST
            continue
        stop = first if at < first else blocks - LATE
        starts.append((at, min(CHUNK, stop - at)))
        at += starts[-1][1]
    return (first, FIRST), starts + [(0, LATE), (blocks - LATE, LATE)]


def job_list(blocks):
    first, chunks = chunk_plan(blocks)
    rows = blocks * BLK
    own = [("own", start, size, start * BLK, blocks + start - SHIFT) for start, size in chunks]
    extra = [
        ("left", first[0], first[1], rows, first[0] - SHIFT),
        ("right", first[0], first[1], rows + FIRST * BLK, 2 * blocks + first[0] - SHIFT),
        ("first", first[0], first[1], first[0] * BLK, blocks + first[0] - SHIFT),
    ]
    return own[:FOREIGN_AT] + extra + own[FOREIGN_AT:]


def mixed_kernel(
    jobs, blocks, groups, var_size,
    z_ref, band_ref, mix_ref, ld_ref, start_ref, count_ref, ext_ref, late_ref, ldv_ref, part_ref,
    zb, bandv, w, gathered, mv, results, starts, counts,
    z_sem, ld_sem, win_sem, band_sem, mix_sem, edge_send, edge_recv, in_send, in_recv, out_send, out_recv,
    first_send, first_recv, halo_send, halo_recv,
):
    t = lax.axis_index("trait")
    g = lax.axis_index("sec") * var_size + lax.axis_index("var")
    x_peer = t + 1 - 2 * lax.rem(t, 2)
    y_peer = t + 2 - 4 * (t // 2)
    far_peer = x_peer + y_peer - t
    peers = (t, x_peer, y_peer, far_peer)
    others = range(1, len(peers))
    right = {"sec": (g + 1) // var_size, "var": lax.rem(g + 1, var_size)}
    left_g = lax.rem(g + groups - 1, groups)
    left = {"sec": left_g // var_size, "var": lax.rem(left_g, var_size)}
    has_left, has_right = g > 0, g < groups - 1
    rows = blocks * BLK
    count_jobs = len(jobs)
    order = range(count_jobs)
    first_c = [c for c in order if jobs[c][0] == "first"][0]

    barrier = pltpu.get_barrier_semaphore()

    def greet(device):
        pl.semaphore_signal(barrier, inc=1, device_id=device, device_id_type=MESH)

    for j in others:
        greet({"trait": peers[j]})
    pl.when(has_left)(lambda: greet(left))
    pl.when(has_right)(lambda: greet(right))

    def remote(src, dst, send, recv, device):
        return pltpu.make_async_remote_copy(
            src_ref=src, dst_ref=dst, send_sem=send, recv_sem=recv,
            device_id=device, device_id_type=MESH,
        )

    def gated(c, act):
        kind = jobs[c][0]
        if kind == "left":
            pl.when(has_left)(act)
        elif kind == "right":
            pl.when(has_right)(act)
        else:
            act()

    def is_own(c):
        return jobs[c][0] in ("own", "first")

    load_z = pltpu.make_async_copy(z_ref, zb.at[pl.ds(BLK, rows)], z_sem)
    load_z.start()

    def load_band(c):
        part = pl.ds(jobs[c][1], jobs[c][2])
        return pltpu.make_async_copy(band_ref.at[part], bandv.at[part], band_sem.at[c])

    to_whiten = [first_c] + [c for c in order if jobs[c][0] == "own"]
    for c in to_whiten:
        load_band(c).start()
    load_mix = [
        pltpu.make_async_copy(
            mix_ref.at[
                pl.ds(pl.multiple_of(taken * BLK, BLK), BLK), pl.ds(pl.multiple_of(given * BLK, BLK), BLK)
            ],
            mv.at[pl.ds(i * BLK, BLK), pl.ds(j * BLK, BLK)],
            mix_sem.at[i, j],
        )
        for i, taken in enumerate(peers)
        for j, given in enumerate(peers)
    ]
    for copy in load_mix:
        copy.start()
    load_ld = pltpu.make_async_copy(ld_ref, ldv_ref, ld_sem)
    load_windows = [
        pltpu.make_async_copy(start_ref, starts, win_sem.at[0]),
        pltpu.make_async_copy(count_ref, counts, win_sem.at[1]),
    ]

    @pl.when(jnp.logical_not(has_left))
    def _():
        zb[pl.ds(0, BLK), :] = jnp.zeros((BLK, BLK), zb.dtype)

    @pl.when(jnp.logical_not(has_right))
    def _():
        zb[pl.ds(rows + BLK, BLK), :] = jnp.zeros((BLK, BLK), zb.dtype)

    edge_right = remote(
        z_ref.at[pl.ds(rows - BLK, BLK)], zb.at[pl.ds(0, BLK)], edge_send.at[0], edge_recv.at[0], right
    )
    edge_left = remote(
        z_ref.at[pl.ds(0, BLK)], zb.at[pl.ds(rows + BLK, BLK)], edge_send.at[1], edge_recv.at[1], left
    )

    def whiten(c):
        _, start, size, _, _ = jobs[c]
        load_band(c).wait()
        if start + size == blocks:
            pl.when(has_right)(edge_left.wait_recv)
        if start == 0:
            pl.when(has_left)(edge_right.wait_recv)

        def one(i, carry):
            b = start + i
            row = pl.multiple_of(b * BLK, BLK)
            sums = jnp.dot(bandv[b], zb[pl.ds(row, 3 * BLK), :], preferred_element_type=jnp.float32)
            w[pl.ds(row, BLK), :] = sums.astype(w.dtype)
            return carry

        lax.fori_loop(0, size, one, 0, unroll=True)

    first_at = pl.ds(jobs[first_c][3], FIRST * BLK)
    first_right = remote(
        w.at[first_at], w.at[pl.ds(rows, FIRST * BLK)], first_send.at[0], first_recv.at[0], right
    )
    first_left = remote(
        w.at[first_at], w.at[pl.ds(rows + FIRST * BLK, FIRST * BLK)], first_send.at[1], first_recv.at[1], left
    )

    def part_rows(c):
        return jobs[c][2] * BLK // len(peers)

    def part_of(c, peer):
        part = part_rows(c)
        return pl.ds(pl.multiple_of(jobs[c][3] + peer * part, part), part)

    def land_of(c, peer):
        part = part_rows(c)
        if part % BLK == 0:
            return ext_ref.at[jobs[c][4] + peer]
        row = peer * part
        return ext_ref.at[jobs[c][4] + row // BLK, pl.ds(pl.multiple_of(lax.rem(row, BLK), part), part)]

    def share_of(c):
        return pl.ds(jobs[c][3] // len(peers), part_rows(c))

    def sends_in(c):
        return [
            remote(
                w.at[part_of(c, peers[j])], gathered.at[j - 1, share_of(c)],
                in_send.at[j - 1, c], in_recv.at[j - 1, c], {"trait": peers[j]},
            )
            for j in others
        ]

    def sends_out(c):
        return [
            remote(
                results.at[j - 1, share_of(c)], land_of(c, t),
                out_send.at[j - 1, c], out_recv.at[j - 1, c], {"trait": peers[j]},
            )
            for j in others
        ]

    def arrivals(c):
        return [
            remote(
                results.at[j - 1, share_of(c)], land_of(c, peers[j]),
                out_send.at[j - 1, c], out_recv.at[j - 1, c], {"trait": peers[j]},
            )
            for j in others
        ]

    def start_in(c):
        def act():
            if jobs[c][0] == "left":
                first_right.wait_recv()
            if jobs[c][0] == "right":
                first_left.wait_recv()
            for copy in sends_in(c):
                copy.start()

        gated(c, act)

    def mix(c):
        def act():
            for copy in sends_in(c):
                copy.wait_recv()
            all_traits = jnp.concatenate(
                [w[part_of(c, t), :]] + [gathered[j - 1, share_of(c), :] for j in others], axis=1
            )
            sums = jnp.dot(all_traits, mv[...], preferred_element_type=jnp.float32).astype(w.dtype)
            land_of(c, t)[...] = sums[:, :BLK]
            for j in others:
                results[j - 1, share_of(c), :] = sums[:, j * BLK : (j + 1) * BLK]
            for copy in sends_out(c):
                copy.start()

        gated(c, act)

    def halo(c, side, offset, length, slot):
        _, start, size, _, land = jobs[c]
        if side == 0:
            place, at = (late_ref, start) if start < LATE else (ext_ref, start - SHIFT)
        elif start >= blocks - LATE:
            place, at = late_ref, 2 * LATE + start - blocks
        else:
            place, at = ext_ref, 2 * blocks + start - SHIFT
        return remote(
            ext_ref.at[pl.ds(land + offset, length)], place.at[pl.ds(at + offset, length)],
            halo_send.at[side, slot, c], halo_recv.at[side, slot, c], right if side == 0 else left,
        )

    own_jobs = [c for c in order if jobs[c][0] == "own"]
    by_parts = own_jobs[:BY_PARTS]
    tails = own_jobs[-2:]

    def piece(c, side, j):
        return halo(c, side, peers[j], 1, j)

    def pieces(c, side):
        if c in by_parts:
            return [piece(c, side, j) for j in range(len(peers))]
        return [halo(c, side, 0, jobs[c][2], 0)]

    def is_late(c, side):
        return (side == 0 and jobs[c][1] < LATE) or (side == 1 and jobs[c][1] >= blocks - LATE)

    def send_halo(c, side):
        for copy in pieces(c, side):
            pl.when(has_right if side == 0 else has_left)(copy.start)

    near = 3 * blocks - 2 * LATE
    for b in (0, near + 1):
        ext_ref[b] = jnp.zeros((BLK, BLK), ext_ref.dtype)
    load_z.wait()
    whiten(first_c)
    pending = [c for c in to_whiten if c != first_c]

    def whiten_upto(i):
        if i < count_jobs and jobs[i][0] == "own" and i in pending:
            pending.remove(i)
            whiten(i)

    for i in range(AHEAD):
        whiten_upto(i)
    pl.semaphore_wait(barrier, len(others) + has_left.astype(jnp.int32) + has_right.astype(jnp.int32))
    pl.when(has_right)(first_right.start)
    pl.when(has_left)(first_left.start)
    for c in order[:AHEAD]:
        start_in(c)
    pl.when(has_right)(edge_right.start)
    pl.when(has_left)(edge_left.start)
    load_ld.start()
    for copy in load_windows:
        copy.start()
    whiten_upto(AHEAD)
    for copy in load_mix:
        copy.wait()

    def settle(c):
        def act():
            for j, copy in zip(others, arrivals(c)):
                copy.wait_recv()
                if c in by_parts:
                    pl.when(has_right)(piece(c, 0, j).start)
                    pl.when(has_left)(piece(c, 1, j).start)

        gated(c, act)
        if jobs[c][0] != "own" or c in by_parts:
            return
        if c == tails[0]:
            send_halo(c, 1)
        elif c == tails[1]:
            send_halo(c, 0)
            send_halo(tails[0], 0)
            send_halo(c, 1)
        else:
            send_halo(c, 0)
            send_halo(c, 1)

    for i in range(count_jobs + LAG):
        if i < count_jobs:
            mix(i)
            if i in by_parts:
                pl.when(has_right)(piece(i, 0, 0).start)
                pl.when(has_left)(piece(i, 1, 0).start)
        if i + AHEAD < count_jobs:
            start_in(i + AHEAD)
        if i >= LAG:
            settle(i - LAG)
        whiten_upto(i + AHEAD + 1)

    def wait_halos(late):
        @pl.when(has_right)
        def _():
            for c in own_jobs:
                if is_late(c, 1) == late:
                    for copy in pieces(c, 1):
                        copy.wait_recv()

        @pl.when(has_left)
        def _():
            for c in own_jobs:
                if is_late(c, 0) == late:
                    for copy in pieces(c, 0):
                        copy.wait_recv()

    load_ld.wait()
    for copy in load_windows:
        copy.wait()
    wait_halos(False)

    def early(i, carry):
        for k in range(GROUP):
            u = i * GROUP + k
            at = starts[u] - (g - 1) * blocks - SHIFT
            many = counts[u]
            parts = []
            for s in range(WIN):
                b = jnp.clip(at + s, 0, near + 1)
                if s:
                    b = b * jnp.clip(many - s, 0, 1)
                parts.append(ext_ref[b])
            sums = jnp.dot(ldv_ref[u], jnp.concatenate(parts, axis=0), preferred_element_type=jnp.float32)
            part_ref[u] = sums.astype(part_ref.dtype)
        return carry

    lax.fori_loop(0, part_ref.shape[0] // GROUP, early, 0)

    for c in order:
        def finish(c=c):
            for copy in sends_in(c) + sends_out(c):
                copy.wait_send()

        gated(c, finish)

    @pl.when(has_right)
    def _():
        first_right.wait_send()
        edge_right.wait_send()
        for c in own_jobs:
            for copy in pieces(c, 0):
                copy.wait_send()

    @pl.when(has_left)
    def _():
        first_left.wait_send()
        edge_left.wait_send()
        for c in own_jobs:
            for copy in pieces(c, 1):
                copy.wait_send()

    wait_halos(True)


def mixed_with_neighbours(z_typed, band_inverse, trait_mix, ld_untyped, win_start, win_count, groups, var_size):
    rows = z_typed.shape[0]
    blocks = rows // BLK
    jobs = job_list(blocks)
    peers = trait_mix.shape[0] // BLK
    untyped = ld_untyped.shape[0]
    work = rows + 2 * FIRST * BLK
    count = len(jobs)
    dma = pltpu.SemaphoreType.DMA
    kind = z_typed.dtype
    hbm = pl.BlockSpec(memory_space=pl.ANY)
    vmem = pl.BlockSpec(memory_space=pltpu.VMEM)
    return pl.pallas_call(
        functools.partial(mixed_kernel, jobs, blocks, groups, var_size),
        out_shape=(
            pltpu.VMEM((3 * blocks - 2 * SHIFT, BLK, BLK), kind),
            pltpu.VMEM((2 * LATE, BLK, BLK), kind),
            pltpu.VMEM(ld_untyped.shape, kind),
            pltpu.VMEM((untyped, BLK, BLK), kind),
        ),
        in_specs=[hbm] * 6,
        out_specs=(vmem, vmem, vmem, vmem),
        scratch_shapes=[
            pltpu.VMEM((rows + 2 * BLK, BLK), kind),
            pltpu.VMEM(band_inverse.shape, kind),
            pltpu.VMEM((work, BLK), kind),
            pltpu.VMEM((peers - 1, work // peers, BLK), kind),
            pltpu.VMEM(trait_mix.shape, kind),
            pltpu.VMEM((peers - 1, work // peers, BLK), kind),
            pltpu.SMEM(win_start.shape, win_start.dtype),
            pltpu.SMEM(win_count.shape, win_count.dtype),
            dma, dma, dma((2,)), dma((count,)), dma((peers, peers)),
            dma((2,)), dma((2,)),
            dma((peers - 1, count)), dma((peers - 1, count)),
            dma((peers - 1, count)), dma((peers - 1, count)),
            dma((2,)), dma((2,)),
            dma((2, peers, count)), dma((2, peers, count)),
        ],
        compiler_params=pltpu.CompilerParams(
            collective_id=0, has_side_effects=True, vmem_limit_bytes=32 * 1024 * 1024
        ),
        name="mixed_kernel",
    )(*(
        pltpu.with_memory_space_constraint(v, pltpu.HBM)
        for v in (z_typed, band_inverse, trait_mix, ld_untyped, win_start, win_count)
    ))


def impute_kernel(blocks, var_size, start_ref, count_ref, ext_ref, late_ref, ld_ref, part_ref, out_ref, fixed, sem):
    g = lax.axis_index("sec") * var_size + lax.axis_index("var")
    untyped = part_ref.shape[0]
    near = 3 * blocks - 2 * LATE

    def window(u):
        at = start_ref[u] - (g - 1) * blocks
        many = count_ref[u]
        return at, many, (at < LATE) | (at + many > LATE + near)

    def send(i, carry):
        for k in range(GROUP):
            u = i * GROUP + k
            _, _, touches = window(u)

            @pl.when(jnp.logical_not(touches))
            def _():
                pltpu.make_async_copy(part_ref.at[u], out_ref.at[u], sem).start()
        return carry

    def redo(u, carry):
        at, many, touches = window(u)

        @pl.when(touches)
        def _():
            parts = []
            for s in range(WIN):
                b = at + s
                middle = ext_ref[jnp.clip(b - SHIFT, 0, near + 1)]
                edge = late_ref[jnp.clip(jnp.where(b < LATE, b, b - near), 0, 2 * LATE - 1)]
                block = jnp.where((b < LATE) | (b >= LATE + near), edge, middle)
                parts.append(jnp.where(s < many, block, jnp.zeros_like(block)))
            sums = jnp.dot(ld_ref[u], jnp.concatenate(parts, axis=0), preferred_element_type=jnp.float32)
            fixed[u] = sums.astype(fixed.dtype)
            pltpu.make_async_copy(fixed.at[u], out_ref.at[u], sem).start()
        return carry

    lax.fori_loop(0, untyped // GROUP, send, 0)
    lax.fori_loop(0, untyped, redo, 0)
    pltpu.make_async_copy(part_ref, out_ref, sem).wait()


def impute(ext, late, ld_untyped, part, win_start, win_count, var_size):
    untyped = ld_untyped.shape[0]
    blocks = (ext.shape[0] + 2 * SHIFT) // 3
    cols = ext.shape[2]
    vmem = pl.BlockSpec(memory_space=pltpu.VMEM)
    return pl.pallas_call(
        functools.partial(impute_kernel, blocks, var_size),
        grid_spec=pltpu.PrefetchScalarGridSpec(
            num_scalar_prefetch=2,
            grid=(1,),
            in_specs=[vmem, vmem, vmem, vmem],
            out_specs=pl.BlockSpec(memory_space=pl.ANY),
            scratch_shapes=[pltpu.VMEM((untyped, BLK, cols), ext.dtype), pltpu.SemaphoreType.DMA],
        ),
        out_shape=jax.ShapeDtypeStruct((untyped, BLK, cols), ext.dtype),
        compiler_params=pltpu.CompilerParams(vmem_limit_bytes=24 * 1024 * 1024),
        name="impute_kernel",
    )(win_start, win_count, ext, late, ld_untyped, part)


def on_device(groups, var_size, z_typed, band_inverse, ld_untyped, trait_mix, win_start, win_count):
    ext, late, ld_near, part = mixed_with_neighbours(
        z_typed, band_inverse, trait_mix, ld_untyped, win_start, win_count, groups, var_size
    )
    imputed = impute(ext, late, ld_near, part, win_start, win_count, var_size)
    return imputed.reshape(ld_untyped.shape[0] * BLK, z_typed.shape[1])


def solution(mesh):
    var_size = mesh.shape["var"]
    groups = mesh.shape["sec"] * var_size
    in_specs = (
        P(("sec", "var"), "trait"),
        P(("sec", "var"), None, None),
        P(("sec", "var"), None, None),
        P(),
        P(("sec", "var")),
        P(("sec", "var")),
    )
    return jax.shard_map(
        functools.partial(on_device, groups, var_size),
        mesh=mesh, in_specs=in_specs, out_specs=P(("sec", "var"), "trait"), check_vma=False,
    )
```

```python
import functools

import jax
import jax.numpy as jnp
from jax import lax
from jax.experimental import pallas as pl
from jax.experimental.pallas import tpu as pltpu
from jax.sharding import PartitionSpec as P

BLK = 128
WIN = 4
FIRST = 4
LAST = 4
LATE = FIRST + LAST
CHUNK = 4
HEADS = ()
FIRST_AT = 5
AHEAD = 2
EAGER = 1
BY_PARTS = 2
GROUP = 8
REDO = 4
MESH = pl.DeviceIdType.MESH


def cut(at, stop, sizes=()):
    sizes, out = list(sizes), []
    while at < stop:
        size = min(sizes.pop(0) if sizes else CHUNK, stop - at)
        out.append((at, size))
        at += size
    return out


def job_list(blocks):
    rows = blocks * BLK
    late = blocks - LATE

    def own(kind, chunks):
        return [(kind, at, size, at * BLK, blocks + at) for at, size in chunks]

    def foreign(kind, at, size, side):
        inside = at - late
        return (kind, at, size, rows + (side * FIRST + inside) * BLK, side * LATE + inside)

    first = cut(late, late + FIRST)
    main = own("own", cut(CHUNK, late, HEADS) + cut(0, CHUNK) + cut(late + FIRST, blocks))
    taken = [foreign(kind, at, size, side) for at, size in first for side, kind in enumerate(("left", "right"))]
    return main[:FIRST_AT] + own("first", first) + main[FIRST_AT:] + taken


def mixed_kernel(
    jobs, blocks, groups, var_size,
    z_ref, band_ref, mix_ref, ld_ref, start_ref, count_ref, ext_ref, late_ref, ldv_ref, part_ref,
    zb, bandv, w, gathered, mv, results, starts, counts,
    z_sem, ld_sem, win_sem, band_sem, mix_sem, main_send, side_send, edge_recv, first_recv, in_recv, out_recv, halo_recv,
):
    t = lax.axis_index("trait")
    g = lax.axis_index("sec") * var_size + lax.axis_index("var")
    x_peer = t + 1 - 2 * lax.rem(t, 2)
    y_peer = t + 2 - 4 * (t // 2)
    far_peer = x_peer + y_peer - t
    peers = (t, x_peer, y_peer, far_peer)
    others = range(1, len(peers))
    right = {"sec": (g + 1) // var_size, "var": lax.rem(g + 1, var_size)}
    left_g = lax.rem(g + groups - 1, groups)
    left = {"sec": left_g // var_size, "var": lax.rem(left_g, var_size)}
    has_left, has_right = g > 0, g < groups - 1
    rows = blocks * BLK
    count_jobs = len(jobs)
    order = range(count_jobs)
    own_jobs = [c for c in order if jobs[c][0] == "own"]
    first_jobs = [c for c in order if jobs[c][0] == "first"]
    foreign = [c for c in order if jobs[c][0] in ("left", "right")]
    late = blocks - LATE

    barrier = pltpu.get_barrier_semaphore()

    def greet(device):
        pl.semaphore_signal(barrier, inc=1, device_id=device, device_id_type=MESH)

    def remote(src, dst, send, recv, device):
        return pltpu.make_async_remote_copy(
            src_ref=src, dst_ref=dst, send_sem=send, recv_sem=recv,
            device_id=device, device_id_type=MESH,
        )

    def gated(c, act):
        kind = jobs[c][0]
        if kind == "left":
            pl.when(has_left)(act)
        elif kind == "right":
            pl.when(has_right)(act)
        else:
            act()

    own_first = first_jobs + own_jobs

    def load_band(k):
        group = [first_jobs, own_jobs[:1], own_jobs[1:]][k]
        for c in group:
            part = pl.ds(jobs[c][1], jobs[c][2])
            pltpu.make_async_copy(band_ref.at[part], bandv.at[part], band_sem.at[k]).start()
        return sum(jobs[c][2] for c in group)

    def wait_band(k, size):
        part = pl.ds(0, size)
        pltpu.make_async_copy(band_ref.at[part], bandv.at[part], band_sem.at[k]).wait()

    def load_rows(k, at, stop):
        part = pl.ds(at * BLK, (stop - at) * BLK)
        return pltpu.make_async_copy(z_ref.at[part], zb.at[pl.ds((at + 1) * BLK, (stop - at) * BLK)], z_sem.at[k])

    cuts = [0, late - 1, late + FIRST + 1, blocks]
    load_z = [load_rows(k, *span) for k, span in enumerate(zip(cuts[:-1], cuts[1:]))]
    load_z[1].start()
    band_sizes = [load_band(0)]
    load_z[0].start()
    band_sizes.append(load_band(1))
    load_z[2].start()
    band_sizes.append(load_band(2))

    for j in others:
        greet({"trait": peers[j]})
    pl.when(has_left)(lambda: greet(left))
    pl.when(has_right)(lambda: greet(right))
    load_mix = [
        pltpu.make_async_copy(
            mix_ref.at[
                pl.ds(pl.multiple_of(taken * BLK, BLK), BLK), pl.ds(pl.multiple_of(given * BLK, BLK), BLK)
            ],
            mv.at[pl.ds(i * BLK, BLK), pl.ds(j * BLK, BLK)],
            mix_sem,
        )
        for i, taken in enumerate(peers)
        for j, given in enumerate(peers)
    ]
    load_ld = pltpu.make_async_copy(ld_ref, ldv_ref, ld_sem)
    load_windows = [
        pltpu.make_async_copy(start_ref, starts, win_sem.at[0]),
        pltpu.make_async_copy(count_ref, counts, win_sem.at[1]),
    ]

    @pl.when(jnp.logical_not(has_left))
    def _():
        zb[pl.ds(0, BLK), :] = jnp.zeros((BLK, BLK), zb.dtype)

    @pl.when(jnp.logical_not(has_right))
    def _():
        zb[pl.ds(rows + BLK, BLK), :] = jnp.zeros((BLK, BLK), zb.dtype)

    edge_right = remote(
        z_ref.at[pl.ds(rows - BLK, BLK)], zb.at[pl.ds(0, BLK)], side_send.at[0], edge_recv.at[0], right
    )
    edge_left = remote(
        z_ref.at[pl.ds(0, BLK)], zb.at[pl.ds(rows + BLK, BLK)], side_send.at[1], edge_recv.at[1], left
    )

    def whiten(c):
        _, start, size, _, _ = jobs[c]
        k = 0 if c in first_jobs else 1 if c == own_jobs[0] else 2
        if band_sizes[k]:
            wait_band(k, band_sizes[k])
            band_sizes[k] = 0
        if start + size == blocks:
            pl.when(has_right)(edge_left.wait_recv)
        if start == 0:
            pl.when(has_left)(edge_right.wait_recv)

        def one(i, carry):
            b = start + i
            row = pl.multiple_of(b * BLK, BLK)
            sums = jnp.dot(bandv[b], zb[pl.ds(row, 3 * BLK), :], preferred_element_type=jnp.float32)
            w[pl.ds(row, BLK), :] = sums.astype(w.dtype)
            return carry

        lax.fori_loop(0, size, one, 0, unroll=True)

    def first(c):
        side = 0 if jobs[c][0] == "left" else 1
        at = pl.ds(jobs[c][1] * BLK, jobs[c][2] * BLK)
        return remote(
            w.at[at], w.at[pl.ds(jobs[c][3], jobs[c][2] * BLK)],
            side_send.at[side], first_recv.at[side], (right, left)[side],
        ), (has_right, has_left)[side]

    def part_rows(c):
        return jobs[c][2] * BLK // len(peers)

    def part_of(c, peer):
        part = part_rows(c)
        return pl.ds(pl.multiple_of(jobs[c][3] + peer * part, part), part)

    def view(ref, at, c, peer):
        part = part_rows(c)
        if part == BLK:
            return ref.at[at + peer]
        row = peer * part
        return ref.at[at + row // BLK, pl.ds(pl.multiple_of(lax.rem(row, BLK), part), part)]

    def land_of(c, peer):
        return view(late_ref if c in foreign else ext_ref, jobs[c][4], c, peer)

    def share_of(c):
        return pl.ds(jobs[c][3] // len(peers), part_rows(c))

    def send_sem(c):
        return {"left": side_send.at[1], "right": side_send.at[0]}.get(jobs[c][0], main_send)

    def sends_in(c):
        return [
            remote(
                w.at[part_of(c, peers[j])], gathered.at[j - 1, share_of(c)],
                send_sem(c), in_recv.at[c], {"trait": peers[j]},
            )
            for j in others
        ]

    def sends_out(c):
        return [
            remote(
                results.at[j - 1, share_of(c)], land_of(c, t),
                send_sem(c), out_recv.at[c], {"trait": peers[j]},
            )
            for j in others
        ]

    def await_in(c):
        ref = gathered.at[:, share_of(c)]
        remote(ref, ref, send_sem(c), in_recv.at[c], {"trait": x_peer}).wait_recv()

    def await_out(c):
        ref = results.at[:, share_of(c)]
        remote(ref, ref, send_sem(c), out_recv.at[c], {"trait": x_peer}).wait_recv()

    def start_in(c):
        def act():
            if c in foreign:
                first(c)[0].wait_recv()
            for copy in sends_in(c):
                copy.start()

        gated(c, act)

    def mix(c):
        def act():
            await_in(c)
            all_traits = jnp.concatenate(
                [w[part_of(c, t), :]] + [gathered[j - 1, share_of(c), :] for j in others], axis=1
            )
            sums = jnp.dot(all_traits, mv[...], preferred_element_type=jnp.float32).astype(w.dtype)
            land_of(c, t)[...] = sums[:, :BLK]
            for j in others:
                results[j - 1, share_of(c), :] = sums[:, j * BLK : (j + 1) * BLK]
            for copy in sends_out(c):
                copy.start()

        gated(c, act)

    by_parts = own_jobs[:BY_PARTS]

    def is_late(c):
        return jobs[c][1] >= late

    def halo_at(c, side):
        start = jobs[c][1]
        if is_late(c):
            return late_ref, side * LATE + start - late
        return ext_ref, side * 2 * blocks + start

    def send_halo(c, side, part=None):
        ref, at = halo_at(c, side)
        if part is None:
            source, target = ext_ref.at[pl.ds(jobs[c][4], jobs[c][2])], ref.at[pl.ds(at, jobs[c][2])]
        else:
            source, target = view(ext_ref, jobs[c][4], c, part), view(ref, at, c, part)
        copy = remote(
            source, target, side_send.at[side], halo_recv.at[side, int(is_late(c))], right if side == 0 else left
        )
        pl.when(has_right if side == 0 else has_left)(copy.start)

    def send_halos(c, which):
        for j in which:
            for side in (0, 1):
                send_halo(c, side, None if j is None else peers[j])

    load_z[1].wait()
    pending = list(own_first)

    def whiten_upto(i):
        if i < count_jobs and i in pending:
            pending.remove(i)
            whiten(i)

    for c in first_jobs:
        whiten_upto(c)
    load_z[0].wait()
    for c in range(EAGER):
        whiten_upto(c)
    pl.semaphore_wait(barrier, len(others) + has_left.astype(jnp.int32) + has_right.astype(jnp.int32))
    for c in foreign:
        copy, sends = first(c)
        pl.when(sends)(copy.start)
    for c in range(EAGER):
        start_in(c)
    pl.when(has_right)(edge_right.start)
    pl.when(has_left)(edge_left.start)
    for copy in load_mix:
        copy.start()
    load_z[2].wait()
    for c in range(EAGER, AHEAD):
        whiten_upto(c)
    for c in range(EAGER, AHEAD):
        start_in(c)
    load_ld.start()
    for copy in load_windows:
        copy.start()
    whiten_upto(AHEAD)
    for b in (*range(late, blocks), *range(2 * blocks + late, 3 * blocks + 1)):
        ext_ref[b] = jnp.zeros((BLK, BLK), ext_ref.dtype)
    pltpu.make_async_copy(mix_ref, mv, mix_sem).wait()

    def settle(c):
        gated(c, lambda: await_out(c))
        if c in own_jobs:
            send_halos(c, others if c in by_parts else (None,))

    for i in range(count_jobs + 1):
        if i < count_jobs:
            mix(i)
            if i in by_parts:
                send_halos(i, (0,))
        if i + AHEAD < count_jobs:
            start_in(i + AHEAD)
        if i >= 1 and i - 1 not in foreign:
            settle(i - 1)
        whiten_upto(i + AHEAD + 1)

    def wait_halos(last):
        size = sum(jobs[c][2] for c in own_jobs if is_late(c) == last)
        ref = late_ref.at[pl.ds(0, size)] if last else ext_ref.at[pl.ds(0, size)]
        from_right = remote(ref, ref, side_send.at[1], halo_recv.at[1, int(last)], right)
        from_left = remote(ref, ref, side_send.at[0], halo_recv.at[0, int(last)], left)
        pl.when(has_right)(from_right.wait_recv)
        pl.when(has_left)(from_left.wait_recv)

    load_ld.wait()
    for copy in load_windows:
        copy.wait()
    wait_halos(False)

    nothing = 3 * blocks

    def early(i, carry):
        for k in range(GROUP):
            u = i * GROUP + k
            at = starts[u] - (g - 1) * blocks
            many = counts[u]
            parts = []
            for s in range(WIN):
                b = jnp.clip(at + s, 0, nothing)
                if s:
                    b = nothing + (b - nothing) * jnp.clip(many - s, 0, 1)
                parts.append(ext_ref[b])
            sums = jnp.dot(ldv_ref[u], jnp.concatenate(parts, axis=0), preferred_element_type=jnp.float32)
            part_ref[u] = sums.astype(part_ref.dtype)
        return carry

    lax.fori_loop(0, part_ref.shape[0] // GROUP, early, 0)

    for c in foreign:
        settle(c)

    def sent(size, sem):
        ref = ext_ref.at[pl.ds(0, size)]
        return remote(ref, ref, sem, edge_recv.at[0], right)

    sent(6 * blocks // len(peers), main_send).wait_send()
    side_size = blocks + 1 + 6 * FIRST // len(peers)
    pl.when(has_right)(sent(side_size, side_send.at[0]).wait_send)
    pl.when(has_left)(sent(side_size, side_send.at[1]).wait_send)
    wait_halos(True)


def mixed_with_neighbours(z_typed, band_inverse, trait_mix, ld_untyped, win_start, win_count, groups, var_size):
    rows = z_typed.shape[0]
    blocks = rows // BLK
    jobs = job_list(blocks)
    peers = trait_mix.shape[0] // BLK
    untyped = ld_untyped.shape[0]
    work = rows + 2 * FIRST * BLK
    count = len(jobs)
    dma = pltpu.SemaphoreType.DMA
    kind = z_typed.dtype
    hbm = pl.BlockSpec(memory_space=pl.ANY)
    vmem = pl.BlockSpec(memory_space=pltpu.VMEM)
    return pl.pallas_call(
        functools.partial(mixed_kernel, jobs, blocks, groups, var_size),
        out_shape=(
            pltpu.VMEM((3 * blocks + 1, BLK, BLK), kind),
            pltpu.VMEM((2 * LATE, BLK, BLK), kind),
            pltpu.VMEM(ld_untyped.shape, kind),
            pltpu.VMEM((untyped, BLK, BLK), kind),
        ),
        in_specs=[hbm] * 6,
        out_specs=(vmem, vmem, vmem, vmem),
        scratch_shapes=[
            pltpu.VMEM((rows + 2 * BLK, BLK), kind),
            pltpu.VMEM(band_inverse.shape, kind),
            pltpu.VMEM((work, BLK), kind),
            pltpu.VMEM((peers - 1, work // peers, BLK), kind),
            pltpu.VMEM(trait_mix.shape, kind),
            pltpu.VMEM((peers - 1, work // peers, BLK), kind),
            pltpu.SMEM(win_start.shape, win_start.dtype),
            pltpu.SMEM(win_count.shape, win_count.dtype),
            dma((3,)), dma, dma((2,)), dma((3,)), dma, dma, dma((2,)), dma((2,)), dma((2,)),
            dma((count,)), dma((count,)), dma((2, 2)),
        ],
        compiler_params=pltpu.CompilerParams(
            collective_id=0, has_side_effects=True, vmem_limit_bytes=32 * 1024 * 1024
        ),
        name="mixed_kernel",
    )(*(
        pltpu.with_memory_space_constraint(v, pltpu.HBM)
        for v in (z_typed, band_inverse, trait_mix, ld_untyped, win_start, win_count)
    ))


def impute_kernel(blocks, var_size, start_ref, count_ref, ext_ref, late_ref, ld_ref, part_ref, out_ref, fixed, sem):
    g = lax.axis_index("sec") * var_size + lax.axis_index("var")
    untyped = part_ref.shape[0]
    base = (g - 1) * blocks
    one, zero = jnp.int32(1), jnp.int32(0)
    spans = ((blocks - LATE, blocks), (3 * blocks - LATE, 3 * blocks))
    bounds = [zero] * 4
    for u in range(untyped):
        at = start_ref[u] - base
        for k, (low, high) in enumerate(spans):
            bounds[2 * k] += jnp.where(at + WIN <= low, one, zero)
            bounds[2 * k + 1] += jnp.where(at < high, one, zero)
    groups = untyped // REDO
    a0, a1 = bounds[0] // REDO, (bounds[1] + REDO - 1) // REDO
    b0 = jnp.maximum(a1, bounds[2] // REDO)

    def part_of(ref, i):
        return ref.at[pl.ds(i * REDO, REDO)]

    def keep(i, carry):
        pltpu.make_async_copy(part_of(part_ref, i), part_of(out_ref, i), sem).start()
        return carry

    def redo(i, carry):
        for k in range(REDO):
            u = i * REDO + k
            at = start_ref[u] - base
            many = count_ref[u]
            parts = []
            for s in range(WIN):
                b = at + s
                inside = [(b >= low) & (b < high) for low, high in spans]
                place = jnp.where(inside[0], b - spans[0][0], b - spans[1][0] + LATE)
                edge = late_ref[jnp.clip(place, 0, 2 * LATE - 1)]
                middle = ext_ref[jnp.clip(b, 0, 3 * blocks)]
                block = jnp.where(inside[0] | inside[1], edge, middle)
                parts.append(jnp.where(s < many, block, jnp.zeros_like(block)))
            sums = jnp.dot(ld_ref[u], jnp.concatenate(parts, axis=0), preferred_element_type=jnp.float32)
            fixed[u] = sums.astype(fixed.dtype)
        pltpu.make_async_copy(part_of(fixed, i), part_of(out_ref, i), sem).start()
        return carry

    lax.fori_loop(0, a0, keep, 0)
    lax.fori_loop(a1, b0, keep, 0)
    lax.fori_loop(a0, a1, redo, 0)
    lax.fori_loop(b0, groups, redo, 0)
    pltpu.make_async_copy(part_ref, out_ref, sem).wait()


def impute(ext, late, ld_untyped, part, win_start, win_count, var_size):
    untyped = ld_untyped.shape[0]
    blocks = ext.shape[0] // 3
    cols = ext.shape[2]
    vmem = pl.BlockSpec(memory_space=pltpu.VMEM)
    return pl.pallas_call(
        functools.partial(impute_kernel, blocks, var_size),
        grid_spec=pltpu.PrefetchScalarGridSpec(
            num_scalar_prefetch=2,
            grid=(1,),
            in_specs=[vmem, vmem, vmem, vmem],
            out_specs=pl.BlockSpec(memory_space=pl.ANY),
            scratch_shapes=[pltpu.VMEM((untyped, BLK, cols), ext.dtype), pltpu.SemaphoreType.DMA],
        ),
        out_shape=jax.ShapeDtypeStruct((untyped, BLK, cols), ext.dtype),
        compiler_params=pltpu.CompilerParams(vmem_limit_bytes=24 * 1024 * 1024),
        name="impute_kernel",
    )(win_start, win_count, ext, late, ld_untyped, part)


def on_device(groups, var_size, z_typed, band_inverse, ld_untyped, trait_mix, win_start, win_count):
    ext, late, ld_near, part = mixed_with_neighbours(
        z_typed, band_inverse, trait_mix, ld_untyped, win_start, win_count, groups, var_size
    )
    imputed = impute(ext, late, ld_near, part, win_start, win_count, var_size)
    return imputed.reshape(ld_untyped.shape[0] * BLK, z_typed.shape[1])


def solution(mesh):
    var_size = mesh.shape["var"]
    groups = mesh.shape["sec"] * var_size
    in_specs = (
        P(("sec", "var"), "trait"),
        P(("sec", "var"), None, None),
        P(("sec", "var"), None, None),
        P(),
        P(("sec", "var")),
        P(("sec", "var")),
    )
    return jax.shard_map(
        functools.partial(on_device, groups, var_size),
        mesh=mesh, in_specs=in_specs, out_specs=P(("sec", "var"), "trait"), check_vma=False,
    )
```

```python
import functools

import jax
import jax.numpy as jnp
from jax import lax
from jax.experimental import pallas as pl
from jax.experimental.pallas import tpu as pltpu
from jax.sharding import PartitionSpec as P

BLK = 128
WIN = 4
FIRST = 4
LAST = 8
CHUNK = 4
HEADS = ()
FIRST_AT = 5
AHEAD = 2
EAGER = 1
BY_PARTS = 4
GROUP = 8
REDO = 4
DELAY = 1
MESH = pl.DeviceIdType.MESH


def cut(at, stop, sizes=()):
    sizes, out = list(sizes), []
    while at < stop:
        size = min(sizes.pop(0) if sizes else CHUNK, stop - at)
        out.append((at, size))
        at += size
    return out


def job_list(blocks):
    rows = blocks * BLK
    late = blocks - LAST
    begin = late - FIRST

    def own(kind, chunks):
        return [(kind, at, size, at * BLK, blocks + at) for at, size in chunks]

    def foreign(kind, at, size, side):
        return (kind, at, size, rows + (side * FIRST + at - begin) * BLK, side * 2 * blocks + at)

    first = cut(begin, late)
    main = own("own", cut(CHUNK, begin, HEADS) + cut(0, CHUNK) + cut(late, blocks))
    taken = [foreign(kind, at, size, side) for at, size in first for side, kind in enumerate(("left", "right"))]
    return main[:FIRST_AT] + own("first", first) + main[FIRST_AT:] + taken


def mixed_kernel(
    jobs, blocks, groups, var_size,
    z_ref, band_ref, mix_ref, ld_ref, start_ref, count_ref, ext_ref, late_ref, ldv_ref, part_ref,
    zb, bandv, w, gathered, mv, results, starts, counts,
    z_sem, ld_sem, win_sem, band_sem, mix_sem, main_send, side_send, edge_recv, first_recv, in_recv, out_recv, halo_recv,
):
    t = lax.axis_index("trait")
    g = lax.axis_index("sec") * var_size + lax.axis_index("var")
    x_peer = t + 1 - 2 * lax.rem(t, 2)
    y_peer = t + 2 - 4 * (t // 2)
    far_peer = x_peer + y_peer - t
    peers = (t, x_peer, y_peer, far_peer)
    others = range(1, len(peers))
    right = {"sec": (g + 1) // var_size, "var": lax.rem(g + 1, var_size)}
    left_g = lax.rem(g + groups - 1, groups)
    left = {"sec": left_g // var_size, "var": lax.rem(left_g, var_size)}
    has_left, has_right = g > 0, g < groups - 1
    rows = blocks * BLK
    count_jobs = len(jobs)
    order = range(count_jobs)
    own_jobs = [c for c in order if jobs[c][0] == "own"]
    first_jobs = [c for c in order if jobs[c][0] == "first"]
    foreign = [c for c in order if jobs[c][0] in ("left", "right")]
    late = blocks - LAST
    begin = late - FIRST

    barrier = pltpu.get_barrier_semaphore()

    def greet(device):
        pl.semaphore_signal(barrier, inc=1, device_id=device, device_id_type=MESH)

    def remote(src, dst, send, recv, device):
        return pltpu.make_async_remote_copy(
            src_ref=src, dst_ref=dst, send_sem=send, recv_sem=recv,
            device_id=device, device_id_type=MESH,
        )

    def gated(c, act):
        kind = jobs[c][0]
        if kind == "left":
            pl.when(has_left)(act)
        elif kind == "right":
            pl.when(has_right)(act)
        else:
            act()

    own_first = first_jobs + own_jobs

    def load_band(k):
        group = [first_jobs, own_jobs[:1], own_jobs[1:]][k]
        for c in group:
            part = pl.ds(jobs[c][1], jobs[c][2])
            pltpu.make_async_copy(band_ref.at[part], bandv.at[part], band_sem.at[k]).start()
        return sum(jobs[c][2] for c in group)

    def wait_band(k, size):
        part = pl.ds(0, size)
        pltpu.make_async_copy(band_ref.at[part], bandv.at[part], band_sem.at[k]).wait()

    def load_rows(k, at, stop):
        part = pl.ds(at * BLK, (stop - at) * BLK)
        return pltpu.make_async_copy(z_ref.at[part], zb.at[pl.ds((at + 1) * BLK, (stop - at) * BLK)], z_sem.at[k])

    cuts = [0, CHUNK - 1, 2 * CHUNK + 1, begin - 1, late + 1, blocks]
    load_z = [load_rows(k, *span) for k, span in enumerate(zip(cuts[:-1], cuts[1:]))]
    load_z[3].start()
    band_sizes = [load_band(0)]
    load_z[1].start()
    band_sizes.append(load_band(1))

    for j in others:
        greet({"trait": peers[j]})
    pl.when(has_left)(lambda: greet(left))
    pl.when(has_right)(lambda: greet(right))
    load_mix = [
        pltpu.make_async_copy(
            mix_ref.at[
                pl.ds(pl.multiple_of(taken * BLK, BLK), BLK), pl.ds(pl.multiple_of(given * BLK, BLK), BLK)
            ],
            mv.at[pl.ds(i * BLK, BLK), pl.ds(j * BLK, BLK)],
            mix_sem,
        )
        for i, taken in enumerate(peers)
        for j, given in enumerate(peers)
    ]
    load_ld = pltpu.make_async_copy(ld_ref, ldv_ref, ld_sem)
    load_windows = [
        pltpu.make_async_copy(start_ref, starts, win_sem.at[0]),
        pltpu.make_async_copy(count_ref, counts, win_sem.at[1]),
    ]

    @pl.when(jnp.logical_not(has_left))
    def _():
        zb[pl.ds(0, BLK), :] = jnp.zeros((BLK, BLK), zb.dtype)

    @pl.when(jnp.logical_not(has_right))
    def _():
        zb[pl.ds(rows + BLK, BLK), :] = jnp.zeros((BLK, BLK), zb.dtype)

    edge_right = remote(
        z_ref.at[pl.ds(rows - BLK, BLK)], zb.at[pl.ds(0, BLK)], side_send.at[0], edge_recv.at[0], right
    )
    edge_left = remote(
        z_ref.at[pl.ds(0, BLK)], zb.at[pl.ds(rows + BLK, BLK)], side_send.at[1], edge_recv.at[1], left
    )

    def whiten(c):
        _, start, size, _, _ = jobs[c]
        k = 0 if c in first_jobs else 1 if c == own_jobs[0] else 2
        if band_sizes[k]:
            wait_band(k, band_sizes[k])
            band_sizes[k] = 0
        if start + size == blocks:
            pl.when(has_right)(edge_left.wait_recv)
        if start == 0:
            pl.when(has_left)(edge_right.wait_recv)

        def one(i, carry):
            b = start + i
            row = pl.multiple_of(b * BLK, BLK)
            sums = jnp.dot(bandv[b], zb[pl.ds(row, 3 * BLK), :], preferred_element_type=jnp.float32)
            w[pl.ds(row, BLK), :] = sums.astype(w.dtype)
            return carry

        lax.fori_loop(0, size, one, 0, unroll=True)

    def first(c):
        side = 0 if jobs[c][0] == "left" else 1
        at = pl.ds(jobs[c][1] * BLK, jobs[c][2] * BLK)
        return remote(
            w.at[at], w.at[pl.ds(jobs[c][3], jobs[c][2] * BLK)],
            side_send.at[side], first_recv.at[foreign.index(c)], (right, left)[side],
        ), (has_right, has_left)[side]

    def part_rows(c):
        return jobs[c][2] * BLK // len(peers)

    def part_of(c, peer):
        part = part_rows(c)
        return pl.ds(pl.multiple_of(jobs[c][3] + peer * part, part), part)

    def view(ref, at, c, peer):
        part = part_rows(c)
        if part == BLK:
            return ref.at[at + peer]
        row = peer * part
        return ref.at[at + row // BLK, pl.ds(pl.multiple_of(lax.rem(row, BLK), part), part)]

    def land_of(c, peer):
        return view(ext_ref, jobs[c][4], c, peer)

    def share_of(c):
        return pl.ds(jobs[c][3] // len(peers), part_rows(c))

    def send_sem(c):
        return {"left": side_send.at[1], "right": side_send.at[0]}.get(jobs[c][0], main_send)

    def sends_in(c):
        return [
            remote(
                w.at[part_of(c, peers[j])], gathered.at[j - 1, share_of(c)],
                send_sem(c), in_recv.at[c], {"trait": peers[j]},
            )
            for j in others
        ]

    def sends_out(c):
        return [
            remote(
                results.at[j - 1, share_of(c)], land_of(c, t),
                send_sem(c), out_recv.at[c], {"trait": peers[j]},
            )
            for j in others
        ]

    def await_in(c):
        ref = gathered.at[:, share_of(c)]
        remote(ref, ref, send_sem(c), in_recv.at[c], {"trait": x_peer}).wait_recv()

    def await_out(c):
        ref = results.at[:, share_of(c)]
        remote(ref, ref, send_sem(c), out_recv.at[c], {"trait": x_peer}).wait_recv()

    def start_in(c):
        def act():
            if c in foreign:
                first(c)[0].wait_recv()
            for copy in sends_in(c):
                copy.start()

        gated(c, act)

    def mix(c):
        def act():
            await_in(c)
            all_traits = jnp.concatenate(
                [w[part_of(c, t), :]] + [gathered[j - 1, share_of(c), :] for j in others], axis=1
            )
            sums = jnp.dot(all_traits, mv[...], preferred_element_type=jnp.float32).astype(w.dtype)
            land_of(c, t)[...] = sums[:, :BLK]
            for j in others:
                results[j - 1, share_of(c), :] = sums[:, j * BLK : (j + 1) * BLK]
            for copy in sends_out(c):
                copy.start()

        gated(c, act)

    by_parts = own_jobs[:BY_PARTS]

    def is_late(c):
        return jobs[c][1] >= late

    def halo_at(c, side):
        start = jobs[c][1]
        if is_late(c):
            return late_ref, side * LAST + start - late
        return ext_ref, side * 2 * blocks + start

    def send_halo(c, side, part):
        ref, at = halo_at(c, side)
        if part is None:
            source, target = ext_ref.at[pl.ds(jobs[c][4], jobs[c][2])], ref.at[pl.ds(at, jobs[c][2])]
        else:
            source, target = view(ext_ref, jobs[c][4], c, part), view(ref, at, c, part)
        copy = remote(
            source, target, side_send.at[side], halo_recv.at[side, int(is_late(c))], right if side == 0 else left
        )
        return copy

    at_end = has_left & (g == var_size - 1)
    held = []

    def send_halos(c, which):
        parts = [None if j is None else peers[j] for j in which]
        for part in parts:
            pl.when(has_right)(send_halo(c, 0, part).start)
            pl.when(has_left & jnp.logical_not(at_end))(send_halo(c, 1, part).start)
        held.append([send_halo(c, 1, part) for part in parts])
        release(DELAY)

    def release(keep):
        while len(held) > keep:
            copies = held.pop(0)

            @pl.when(at_end)
            def _():
                for copy in copies:
                    copy.start()

    load_z[3].wait()
    pending = list(own_first)

    def whiten_upto(i):
        if i < count_jobs and i in pending:
            pending.remove(i)
            whiten(i)

    for c in first_jobs:
        whiten_upto(c)
    for k in (2, 0, 4):
        load_z[k].start()
    band_sizes.append(load_band(2))
    load_z[1].wait()
    for c in range(EAGER):
        whiten_upto(c)
    pl.semaphore_wait(barrier, len(others) + has_left.astype(jnp.int32) + has_right.astype(jnp.int32))
    for c in foreign:
        copy, sends = first(c)
        pl.when(sends)(copy.start)
    for c in range(EAGER):
        start_in(c)
    pl.when(has_right)(edge_right.start)
    pl.when(has_left)(edge_left.start)
    for copy in load_mix:
        copy.start()
    for k in (2, 0, 4):
        load_z[k].wait()
    for c in range(EAGER, AHEAD):
        whiten_upto(c)
    for c in range(EAGER, AHEAD):
        start_in(c)
    load_ld.start()
    for copy in load_windows:
        copy.start()
    whiten_upto(AHEAD)
    for b in (*range(late, blocks), *range(2 * blocks + late, 3 * blocks + 1)):
        ext_ref[b] = jnp.zeros((BLK, BLK), ext_ref.dtype)
    pltpu.make_async_copy(mix_ref, mv, mix_sem).wait()

    def settle(c):
        gated(c, lambda: await_out(c))
        if c in own_jobs:
            send_halos(c, others if c in by_parts else (None,))

    for i in range(count_jobs + 1):
        if i < count_jobs:
            mix(i)
            if i in by_parts:
                send_halos(i, (0,))
        if i + AHEAD < count_jobs:
            start_in(i + AHEAD)
        if i >= 1 and i - 1 not in foreign:
            settle(i - 1)
        whiten_upto(i + AHEAD + 1)

    release(0)

    def wait_halos(last):
        size = sum(jobs[c][2] for c in own_jobs if is_late(c) == last)
        ref = late_ref.at[pl.ds(0, size)] if last else ext_ref.at[pl.ds(0, size)]
        from_right = remote(ref, ref, side_send.at[1], halo_recv.at[1, int(last)], right)
        from_left = remote(ref, ref, side_send.at[0], halo_recv.at[0, int(last)], left)
        pl.when(has_right)(from_right.wait_recv)
        pl.when(has_left)(from_left.wait_recv)

    for c in foreign:
        settle(c)
    load_ld.wait()
    for copy in load_windows:
        copy.wait()
    wait_halos(False)

    nothing = 3 * blocks

    def early(i, carry):
        for k in range(GROUP):
            u = i * GROUP + k
            at = starts[u] - (g - 1) * blocks
            many = counts[u]
            parts = []
            for s in range(WIN):
                b = jnp.clip(at + s, 0, nothing)
                if s:
                    b = nothing + (b - nothing) * jnp.clip(many - s, 0, 1)
                parts.append(ext_ref[b])
            sums = jnp.dot(ldv_ref[u], jnp.concatenate(parts, axis=0), preferred_element_type=jnp.float32)
            part_ref[u] = sums.astype(part_ref.dtype)
        return carry

    lax.fori_loop(0, part_ref.shape[0] // GROUP, early, 0)

    def sent(size, sem):
        ref = ext_ref.at[pl.ds(0, size)]
        return remote(ref, ref, sem, edge_recv.at[0], right)

    sent(6 * blocks // len(peers), main_send).wait_send()
    side_size = blocks + 1 + 6 * FIRST // len(peers)
    pl.when(has_right)(sent(side_size, side_send.at[0]).wait_send)
    pl.when(has_left)(sent(side_size, side_send.at[1]).wait_send)
    wait_halos(True)


def mixed_with_neighbours(z_typed, band_inverse, trait_mix, ld_untyped, win_start, win_count, groups, var_size):
    rows = z_typed.shape[0]
    blocks = rows // BLK
    jobs = job_list(blocks)
    peers = trait_mix.shape[0] // BLK
    untyped = ld_untyped.shape[0]
    work = rows + 2 * FIRST * BLK
    count = len(jobs)
    taken = sum(job[0] in ("left", "right") for job in jobs)
    dma = pltpu.SemaphoreType.DMA
    kind = z_typed.dtype
    hbm = pl.BlockSpec(memory_space=pl.ANY)
    vmem = pl.BlockSpec(memory_space=pltpu.VMEM)
    return pl.pallas_call(
        functools.partial(mixed_kernel, jobs, blocks, groups, var_size),
        out_shape=(
            pltpu.VMEM((3 * blocks + 1, BLK, BLK), kind),
            pltpu.VMEM((2 * LAST, BLK, BLK), kind),
            pltpu.VMEM(ld_untyped.shape, kind),
            pltpu.VMEM((untyped, BLK, BLK), kind),
        ),
        in_specs=[hbm] * 6,
        out_specs=(vmem, vmem, vmem, vmem),
        scratch_shapes=[
            pltpu.VMEM((rows + 2 * BLK, BLK), kind),
            pltpu.VMEM(band_inverse.shape, kind),
            pltpu.VMEM((work, BLK), kind),
            pltpu.VMEM((peers - 1, work // peers, BLK), kind),
            pltpu.VMEM(trait_mix.shape, kind),
            pltpu.VMEM((peers - 1, work // peers, BLK), kind),
            pltpu.SMEM(win_start.shape, win_start.dtype),
            pltpu.SMEM(win_count.shape, win_count.dtype),
            dma((5,)), dma, dma((2,)), dma((3,)), dma, dma, dma((2,)), dma((2,)), dma((taken,)),
            dma((count,)), dma((count,)), dma((2, 2)),
        ],
        compiler_params=pltpu.CompilerParams(
            collective_id=0, has_side_effects=True, vmem_limit_bytes=32 * 1024 * 1024
        ),
        name="mixed_kernel",
    )(*(
        pltpu.with_memory_space_constraint(v, pltpu.HBM)
        for v in (z_typed, band_inverse, trait_mix, ld_untyped, win_start, win_count)
    ))


def impute_kernel(blocks, var_size, start_ref, count_ref, ext_ref, late_ref, ld_ref, part_ref, out_ref, fixed, sem):
    g = lax.axis_index("sec") * var_size + lax.axis_index("var")
    untyped = part_ref.shape[0]
    base = (g - 1) * blocks
    one, zero = jnp.int32(1), jnp.int32(0)
    spans = ((blocks - LAST, blocks), (3 * blocks - LAST, 3 * blocks))
    bounds = [zero] * 4
    for u in range(untyped):
        at = start_ref[u] - base
        for k, (low, high) in enumerate(spans):
            bounds[2 * k] += jnp.where(at + WIN <= low, one, zero)
            bounds[2 * k + 1] += jnp.where(at < high, one, zero)
    groups = untyped // REDO
    a0, a1 = bounds[0] // REDO, (bounds[1] + REDO - 1) // REDO
    b0 = jnp.maximum(a1, bounds[2] // REDO)

    def part_of(ref, i):
        return ref.at[pl.ds(i * REDO, REDO)]

    def keep(i, carry):
        pltpu.make_async_copy(part_of(part_ref, i), part_of(out_ref, i), sem).start()
        return carry

    def redo(i, carry):
        for k in range(REDO):
            u = i * REDO + k
            at = start_ref[u] - base
            many = count_ref[u]
            parts = []
            for s in range(WIN):
                b = at + s
                inside = [(b >= low) & (b < high) for low, high in spans]
                place = jnp.where(inside[0], b - spans[0][0], b - spans[1][0] + LAST)
                edge = late_ref[jnp.clip(place, 0, 2 * LAST - 1)]
                middle = ext_ref[jnp.clip(b, 0, 3 * blocks)]
                block = jnp.where(inside[0] | inside[1], edge, middle)
                parts.append(jnp.where(s < many, block, jnp.zeros_like(block)))
            sums = jnp.dot(ld_ref[u], jnp.concatenate(parts, axis=0), preferred_element_type=jnp.float32)
            fixed[u] = sums.astype(fixed.dtype)
        pltpu.make_async_copy(part_of(fixed, i), part_of(out_ref, i), sem).start()
        return carry

    lax.fori_loop(0, a0, keep, 0)
    lax.fori_loop(a1, b0, keep, 0)
    lax.fori_loop(a0, a1, redo, 0)
    lax.fori_loop(b0, groups, redo, 0)
    pltpu.make_async_copy(part_ref, out_ref, sem).wait()


def impute(ext, late, ld_untyped, part, win_start, win_count, var_size):
    untyped = ld_untyped.shape[0]
    blocks = ext.shape[0] // 3
    cols = ext.shape[2]
    vmem = pl.BlockSpec(memory_space=pltpu.VMEM)
    return pl.pallas_call(
        functools.partial(impute_kernel, blocks, var_size),
        grid_spec=pltpu.PrefetchScalarGridSpec(
            num_scalar_prefetch=2,
            grid=(1,),
            in_specs=[vmem, vmem, vmem, vmem],
            out_specs=pl.BlockSpec(memory_space=pl.ANY),
            scratch_shapes=[pltpu.VMEM((untyped, BLK, cols), ext.dtype), pltpu.SemaphoreType.DMA],
        ),
        out_shape=jax.ShapeDtypeStruct((untyped, BLK, cols), ext.dtype),
        compiler_params=pltpu.CompilerParams(vmem_limit_bytes=24 * 1024 * 1024),
        name="impute_kernel",
    )(win_start, win_count, ext, late, ld_untyped, part)


def on_device(groups, var_size, z_typed, band_inverse, ld_untyped, trait_mix, win_start, win_count):
    ext, late, ld_near, part = mixed_with_neighbours(
        z_typed, band_inverse, trait_mix, ld_untyped, win_start, win_count, groups, var_size
    )
    imputed = impute(ext, late, ld_near, part, win_start, win_count, var_size)
    return imputed.reshape(ld_untyped.shape[0] * BLK, z_typed.shape[1])


def solution(mesh):
    var_size = mesh.shape["var"]
    groups = mesh.shape["sec"] * var_size
    in_specs = (
        P(("sec", "var"), "trait"),
        P(("sec", "var"), None, None),
        P(("sec", "var"), None, None),
        P(),
        P(("sec", "var")),
        P(("sec", "var")),
    )
    return jax.shard_map(
        functools.partial(on_device, groups, var_size),
        mesh=mesh, in_specs=in_specs, out_specs=P(("sec", "var"), "trait"), check_vma=False,
    )
```

```python
import functools

import jax
import jax.numpy as jnp
from jax import lax
from jax.experimental import pallas as pl
from jax.experimental.pallas import tpu as pltpu
from jax.sharding import PartitionSpec as P

BLK = 128
WIN = 4
FIRST = 4
LAST = 8
FOREIGN_LATE = 0
LATE = LAST + FOREIGN_LATE * FIRST
CHUNK = 4
HEADS = ()
FIRST_AT = 5
AHEAD = 2
EAGER = 1
BY_PARTS = 4
GROUP = 8
REDO = 8
DELAY = 1
MESH = pl.DeviceIdType.MESH


def cut(at, stop, sizes=()):
    sizes, out = list(sizes), []
    while at < stop:
        size = min(sizes.pop(0) if sizes else CHUNK, stop - at)
        out.append((at, size))
        at += size
    return out


def job_list(blocks):
    rows = blocks * BLK
    late = blocks - LAST
    begin = late - FIRST

    def own(kind, chunks):
        return [(kind, at, size, at * BLK, blocks + at) for at, size in chunks]

    def foreign(kind, at, size, side):
        land = side * LATE + at - (blocks - LATE) if FOREIGN_LATE else side * 2 * blocks + at
        return (kind, at, size, rows + (side * FIRST + at - begin) * BLK, land)

    first = cut(begin, late)
    main = own("own", cut(CHUNK, begin, HEADS) + cut(0, CHUNK) + cut(late, blocks))
    taken = [foreign(kind, at, size, side) for at, size in first for side, kind in enumerate(("left", "right"))]
    return main[:FIRST_AT] + own("first", first) + main[FIRST_AT:] + taken


def mixed_kernel(
    jobs, blocks, groups, var_size,
    z_ref, band_ref, mix_ref, ld_ref, start_ref, count_ref, ext_ref, ldv_ref, part_ref, starts, counts, touched,
    zb, bandv, w, gathered, mv, results, late_ref,
    z_sem, ld_sem, win_sem, band_sem, mix_sem, main_send, side_send, edge_recv, first_recv, in_recv, out_recv, halo_recv,
):
    t = lax.axis_index("trait")
    g = lax.axis_index("sec") * var_size + lax.axis_index("var")
    x_peer = t + 1 - 2 * lax.rem(t, 2)
    y_peer = t + 2 - 4 * (t // 2)
    far_peer = x_peer + y_peer - t
    peers = (t, x_peer, y_peer, far_peer)
    others = range(1, len(peers))
    right = {"sec": (g + 1) // var_size, "var": lax.rem(g + 1, var_size)}
    left_g = lax.rem(g + groups - 1, groups)
    left = {"sec": left_g // var_size, "var": lax.rem(left_g, var_size)}
    has_left, has_right = g > 0, g < groups - 1
    rows = blocks * BLK
    count_jobs = len(jobs)
    order = range(count_jobs)
    own_jobs = [c for c in order if jobs[c][0] == "own"]
    first_jobs = [c for c in order if jobs[c][0] == "first"]
    foreign = [c for c in order if jobs[c][0] in ("left", "right")]
    late = blocks - LAST
    begin = late - FIRST

    barrier = pltpu.get_barrier_semaphore()

    def greet(device):
        pl.semaphore_signal(barrier, inc=1, device_id=device, device_id_type=MESH)

    for j in others:
        greet({"trait": peers[j]})
    pl.when(has_left)(lambda: greet(left))
    pl.when(has_right)(lambda: greet(right))

    def remote(src, dst, send, recv, device):
        return pltpu.make_async_remote_copy(
            src_ref=src, dst_ref=dst, send_sem=send, recv_sem=recv,
            device_id=device, device_id_type=MESH,
        )

    def gated(c, act):
        kind = jobs[c][0]
        if kind == "left":
            pl.when(has_left)(act)
        elif kind == "right":
            pl.when(has_right)(act)
        else:
            act()

    own_first = first_jobs + own_jobs

    def load_band(k):
        group = [first_jobs, own_jobs[:1], own_jobs[1:]][k]
        for c in group:
            part = pl.ds(jobs[c][1], jobs[c][2])
            pltpu.make_async_copy(band_ref.at[part], bandv.at[part], band_sem.at[k]).start()
        return sum(jobs[c][2] for c in group)

    def wait_band(k, size):
        part = pl.ds(0, size)
        pltpu.make_async_copy(band_ref.at[part], bandv.at[part], band_sem.at[k]).wait()

    def load_rows(k, at, stop):
        part = pl.ds(at * BLK, (stop - at) * BLK)
        return pltpu.make_async_copy(z_ref.at[part], zb.at[pl.ds((at + 1) * BLK, (stop - at) * BLK)], z_sem.at[k])

    cuts = [0, CHUNK - 1, 2 * CHUNK + 1, begin - 1, late + 1, blocks]
    load_z = [load_rows(k, *span) for k, span in enumerate(zip(cuts[:-1], cuts[1:]))]
    load_z[3].start()
    band_sizes = [load_band(0)]
    load_z[1].start()
    band_sizes.append(load_band(1))

    load_mix = [
        pltpu.make_async_copy(
            mix_ref.at[
                pl.ds(pl.multiple_of(taken * BLK, BLK), BLK), pl.ds(pl.multiple_of(given * BLK, BLK), BLK)
            ],
            mv.at[pl.ds(i * BLK, BLK), pl.ds(j * BLK, BLK)],
            mix_sem,
        )
        for i, taken in enumerate(peers)
        for j, given in enumerate(peers)
    ]
    load_ld = pltpu.make_async_copy(ld_ref, ldv_ref, ld_sem)
    load_windows = [
        pltpu.make_async_copy(start_ref, starts, win_sem.at[0]),
        pltpu.make_async_copy(count_ref, counts, win_sem.at[1]),
    ]

    @pl.when(jnp.logical_not(has_left))
    def _():
        zb[pl.ds(0, BLK), :] = jnp.zeros((BLK, BLK), zb.dtype)

    @pl.when(jnp.logical_not(has_right))
    def _():
        zb[pl.ds(rows + BLK, BLK), :] = jnp.zeros((BLK, BLK), zb.dtype)

    edge_right = remote(
        z_ref.at[pl.ds(rows - BLK, BLK)], zb.at[pl.ds(0, BLK)], side_send.at[0], edge_recv.at[0], right
    )
    edge_left = remote(
        z_ref.at[pl.ds(0, BLK)], zb.at[pl.ds(rows + BLK, BLK)], side_send.at[1], edge_recv.at[1], left
    )

    def whiten(c):
        _, start, size, _, _ = jobs[c]
        k = 0 if c in first_jobs else 1 if c == own_jobs[0] else 2
        if band_sizes[k]:
            wait_band(k, band_sizes[k])
            band_sizes[k] = 0
        if start + size == blocks:
            pl.when(has_right)(edge_left.wait_recv)
        if start == 0:
            pl.when(has_left)(edge_right.wait_recv)

        def one(i, carry):
            b = start + i
            row = pl.multiple_of(b * BLK, BLK)
            sums = jnp.dot(bandv[b], zb[pl.ds(row, 3 * BLK), :], preferred_element_type=jnp.float32)
            w[pl.ds(row, BLK), :] = sums.astype(w.dtype)
            return carry

        lax.fori_loop(0, size, one, 0, unroll=True)

    def first(c):
        side = 0 if jobs[c][0] == "left" else 1
        at = pl.ds(jobs[c][1] * BLK, jobs[c][2] * BLK)
        return remote(
            w.at[at], w.at[pl.ds(jobs[c][3], jobs[c][2] * BLK)],
            side_send.at[side], first_recv.at[foreign.index(c)], (right, left)[side],
        ), (has_right, has_left)[side]

    def part_rows(c):
        return jobs[c][2] * BLK // len(peers)

    def part_of(c, peer):
        part = part_rows(c)
        return pl.ds(pl.multiple_of(jobs[c][3] + peer * part, part), part)

    def view(ref, at, c, peer):
        part = part_rows(c)
        if part == BLK:
            return ref.at[at + peer]
        row = peer * part
        return ref.at[at + row // BLK, pl.ds(pl.multiple_of(lax.rem(row, BLK), part), part)]

    def land_of(c, peer):
        return view(late_ref if FOREIGN_LATE and c in foreign else ext_ref, jobs[c][4], c, peer)

    def share_of(c):
        return pl.ds(jobs[c][3] // len(peers), part_rows(c))

    def send_sem(c):
        return {"left": side_send.at[1], "right": side_send.at[0]}.get(jobs[c][0], main_send)

    def sends_in(c):
        return [
            remote(
                w.at[part_of(c, peers[j])], gathered.at[j - 1, share_of(c)],
                send_sem(c), in_recv.at[c], {"trait": peers[j]},
            )
            for j in others
        ]

    def sends_out(c):
        return [
            remote(
                results.at[j - 1, share_of(c)], land_of(c, t),
                send_sem(c), out_recv.at[c], {"trait": peers[j]},
            )
            for j in others
        ]

    def await_in(c):
        ref = gathered.at[:, share_of(c)]
        remote(ref, ref, send_sem(c), in_recv.at[c], {"trait": x_peer}).wait_recv()

    def await_out(c):
        ref = results.at[:, share_of(c)]
        remote(ref, ref, send_sem(c), out_recv.at[c], {"trait": x_peer}).wait_recv()

    def start_in(c):
        def act():
            if c in foreign:
                first(c)[0].wait_recv()
            for copy in sends_in(c):
                copy.start()

        gated(c, act)

    def mix(c):
        def act():
            await_in(c)
            all_traits = jnp.concatenate(
                [w[part_of(c, t), :]] + [gathered[j - 1, share_of(c), :] for j in others], axis=1
            )
            sums = jnp.dot(all_traits, mv[...], preferred_element_type=jnp.float32).astype(w.dtype)
            land_of(c, t)[...] = sums[:, :BLK]
            for j in others:
                results[j - 1, share_of(c), :] = sums[:, j * BLK : (j + 1) * BLK]
            for copy in sends_out(c):
                copy.start()

        gated(c, act)

    by_parts = own_jobs[:BY_PARTS]

    def is_late(c):
        return jobs[c][1] >= late

    def halo_at(c, side):
        start = jobs[c][1]
        if is_late(c):
            return late_ref, side * LATE + start - (blocks - LATE)
        return ext_ref, side * 2 * blocks + start

    def send_halo(c, side, part):
        ref, at = halo_at(c, side)
        if part is None:
            source, target = ext_ref.at[pl.ds(jobs[c][4], jobs[c][2])], ref.at[pl.ds(at, jobs[c][2])]
        else:
            source, target = view(ext_ref, jobs[c][4], c, part), view(ref, at, c, part)
        copy = remote(
            source, target, side_send.at[side], halo_recv.at[side, int(is_late(c))], right if side == 0 else left
        )
        return copy

    at_end = has_left & (g == var_size - 1)
    held = []

    def send_halos(c, which):
        parts = [None if j is None else peers[j] for j in which]
        for part in parts:
            pl.when(has_right)(send_halo(c, 0, part).start)
            pl.when(has_left & jnp.logical_not(at_end))(send_halo(c, 1, part).start)
        held.append([send_halo(c, 1, part) for part in parts])
        release(DELAY)

    def release(keep):
        while len(held) > keep:
            copies = held.pop(0)

            @pl.when(at_end)
            def _():
                for copy in copies:
                    copy.start()

    load_z[3].wait()
    pending = list(own_first)

    def whiten_upto(i):
        if i < count_jobs and i in pending:
            pending.remove(i)
            whiten(i)

    for c in first_jobs:
        whiten_upto(c)
    for k in (2, 0, 4):
        load_z[k].start()
    band_sizes.append(load_band(2))
    load_z[1].wait()
    for c in range(EAGER):
        whiten_upto(c)
    pl.semaphore_wait(barrier, len(others) + has_left.astype(jnp.int32) + has_right.astype(jnp.int32))
    for c in foreign:
        copy, sends = first(c)
        pl.when(sends)(copy.start)
    for c in range(EAGER):
        start_in(c)
    pl.when(has_right)(edge_right.start)
    pl.when(has_left)(edge_left.start)
    for copy in load_mix:
        copy.start()
    for k in (2, 0, 4):
        load_z[k].wait()
    for c in range(EAGER, AHEAD):
        whiten_upto(c)
    for c in range(EAGER, AHEAD):
        start_in(c)
    load_ld.start()
    for copy in load_windows:
        copy.start()
    whiten_upto(AHEAD)
    for b in (*range(blocks - LATE, blocks), *range(3 * blocks - LATE, 3 * blocks + 1)):
        ext_ref[b] = jnp.zeros((BLK, BLK), ext_ref.dtype)
    pltpu.make_async_copy(mix_ref, mv, mix_sem).wait()
    for copy in load_windows:
        copy.wait()
    for i in range(part_ref.shape[0] // REDO):
        found = 0
        for u in range(i * REDO, (i + 1) * REDO):
            at = starts[u] - (g - 1) * blocks
            stop = at + counts[u]
            in_left = jnp.clip(blocks - at, 0, 1) * jnp.clip(stop - (blocks - LATE), 0, 1)
            in_right = jnp.clip(stop - (3 * blocks - LATE), 0, 1)
            found = found + in_left + in_right
        touched[i] = found

    def settle(c):
        gated(c, lambda: await_out(c))
        if c in own_jobs:
            send_halos(c, others if c in by_parts else (None,))

    for i in range(count_jobs + 1):
        if i < count_jobs:
            mix(i)
            if i in by_parts:
                send_halos(i, (0,))
        if i + AHEAD < count_jobs:
            start_in(i + AHEAD)
        if i >= 1 and i - 1 not in foreign:
            settle(i - 1)
        whiten_upto(i + AHEAD + 1)

    release(0)

    def wait_halos(last):
        size = sum(jobs[c][2] for c in own_jobs if is_late(c) == last)
        ref = late_ref.at[pl.ds(0, size)] if last else ext_ref.at[pl.ds(0, size)]
        from_right = remote(ref, ref, side_send.at[1], halo_recv.at[1, int(last)], right)
        from_left = remote(ref, ref, side_send.at[0], halo_recv.at[0, int(last)], left)
        pl.when(has_right)(from_right.wait_recv)
        pl.when(has_left)(from_left.wait_recv)

    if not FOREIGN_LATE:
        for c in foreign:
            settle(c)
    load_ld.wait()
    wait_halos(False)

    nothing = 3 * blocks

    def early(i, carry):
        for k in range(GROUP):
            u = i * GROUP + k
            at = starts[u] - (g - 1) * blocks
            many = counts[u]
            parts = []
            for s in range(WIN):
                b = jnp.clip(at + s, 0, nothing)
                if s:
                    b = nothing + (b - nothing) * jnp.clip(many - s, 0, 1)
                parts.append(ext_ref[b])
            sums = jnp.dot(ldv_ref[u], jnp.concatenate(parts, axis=0), preferred_element_type=jnp.float32)
            part_ref[u] = sums.astype(part_ref.dtype)
        return carry

    lax.fori_loop(0, part_ref.shape[0] // GROUP, early, 0)

    if FOREIGN_LATE:
        for c in foreign:
            settle(c)

    def sent(size, sem):
        ref = ext_ref.at[pl.ds(0, size)]
        return remote(ref, ref, sem, edge_recv.at[0], right)

    sent(6 * blocks // len(peers), main_send).wait_send()
    side_size = blocks + 1 + 6 * FIRST // len(peers)
    pl.when(has_right)(sent(side_size, side_send.at[0]).wait_send)
    pl.when(has_left)(sent(side_size, side_send.at[1]).wait_send)
    wait_halos(True)
    for side in (0, 1):
        for k in range(LATE):
            ext_ref[(2 * side + 1) * blocks - LATE + k] = late_ref[side * LATE + k]


def mixed_with_neighbours(z_typed, band_inverse, trait_mix, ld_untyped, win_start, win_count, groups, var_size):
    rows = z_typed.shape[0]
    blocks = rows // BLK
    jobs = job_list(blocks)
    peers = trait_mix.shape[0] // BLK
    untyped = ld_untyped.shape[0]
    work = rows + 2 * FIRST * BLK
    count = len(jobs)
    taken = sum(job[0] in ("left", "right") for job in jobs)
    dma = pltpu.SemaphoreType.DMA
    kind = z_typed.dtype
    hbm = pl.BlockSpec(memory_space=pl.ANY)
    vmem = pl.BlockSpec(memory_space=pltpu.VMEM)
    smem = pl.BlockSpec(memory_space=pltpu.SMEM)
    return pl.pallas_call(
        functools.partial(mixed_kernel, jobs, blocks, groups, var_size),
        out_shape=(
            pltpu.VMEM((3 * blocks + 1, BLK, BLK), kind),
            pltpu.VMEM(ld_untyped.shape, kind),
            pltpu.VMEM((untyped, BLK, BLK), kind),
            pltpu.SMEM(win_start.shape, win_start.dtype),
            pltpu.SMEM(win_count.shape, win_count.dtype),
            pltpu.SMEM((untyped // REDO,), win_count.dtype),
        ),
        in_specs=[hbm] * 6,
        out_specs=(vmem, vmem, vmem, smem, smem, smem),
        scratch_shapes=[
            pltpu.VMEM((rows + 2 * BLK, BLK), kind),
            pltpu.VMEM(band_inverse.shape, kind),
            pltpu.VMEM((work, BLK), kind),
            pltpu.VMEM((peers - 1, work // peers, BLK), kind),
            pltpu.VMEM(trait_mix.shape, kind),
            pltpu.VMEM((peers - 1, work // peers, BLK), kind),
            pltpu.VMEM((2 * LATE, BLK, BLK), kind),
            dma((5,)), dma, dma((2,)), dma((3,)), dma, dma, dma((2,)), dma((2,)), dma((taken,)),
            dma((count,)), dma((count,)), dma((2, 2)),
        ],
        compiler_params=pltpu.CompilerParams(
            collective_id=0, has_side_effects=True, vmem_limit_bytes=32 * 1024 * 1024
        ),
        name="mixed_kernel",
    )(*(
        pltpu.with_memory_space_constraint(v, pltpu.HBM)
        for v in (z_typed, band_inverse, trait_mix, ld_untyped, win_start, win_count)
    ))


def impute_kernel(blocks, var_size, start_ref, count_ref, touched, ext_ref, ld_ref, part_ref, out_ref, fixed, sem):
    g = lax.axis_index("sec") * var_size + lax.axis_index("var")
    nothing = 3 * blocks

    def send(ref, i):
        part = pl.ds(i * REDO, REDO)
        pltpu.make_async_copy(ref.at[part], out_ref.at[part], sem).start()

    def redo(i):
        for u in range(i * REDO, (i + 1) * REDO):
            at = start_ref[u] - (g - 1) * blocks
            many = count_ref[u]
            parts = []
            for s in range(WIN):
                b = jnp.clip(at + s, 0, nothing)
                parts.append(ext_ref[jnp.where(s < many, b, nothing) if s else b])
            sums = jnp.dot(ld_ref[u], jnp.concatenate(parts, axis=0), preferred_element_type=jnp.float32)
            fixed[u] = sums.astype(fixed.dtype)
        send(fixed, i)

    for i in range(part_ref.shape[0] // REDO):
        pl.when(touched[i] == 0)(functools.partial(send, part_ref, i))
    for i in range(part_ref.shape[0] // REDO):
        pl.when(touched[i] != 0)(functools.partial(redo, i))
    pltpu.make_async_copy(part_ref, out_ref, sem).wait()


def impute(ext, ld_untyped, part, starts, counts, touched, var_size):
    untyped = ld_untyped.shape[0]
    blocks = ext.shape[0] // 3
    cols = ext.shape[2]
    vmem = pl.BlockSpec(memory_space=pltpu.VMEM)
    smem = pl.BlockSpec(memory_space=pltpu.SMEM)
    return pl.pallas_call(
        functools.partial(impute_kernel, blocks, var_size),
        in_specs=[smem, smem, smem, vmem, vmem, vmem],
        out_specs=pl.BlockSpec(memory_space=pl.ANY),
        scratch_shapes=[pltpu.VMEM((untyped, BLK, cols), ext.dtype), pltpu.SemaphoreType.DMA],
        out_shape=jax.ShapeDtypeStruct((untyped, BLK, cols), ext.dtype),
        compiler_params=pltpu.CompilerParams(vmem_limit_bytes=24 * 1024 * 1024),
        name="impute_kernel",
    )(starts, counts, touched, ext, ld_untyped, part)


def on_device(groups, var_size, z_typed, band_inverse, ld_untyped, trait_mix, win_start, win_count):
    ext, ld_near, part, starts, counts, touched = mixed_with_neighbours(
        z_typed, band_inverse, trait_mix, ld_untyped, win_start, win_count, groups, var_size
    )
    imputed = impute(ext, ld_near, part, starts, counts, touched, var_size)
    return imputed.reshape(ld_untyped.shape[0] * BLK, z_typed.shape[1])


def solution(mesh):
    var_size = mesh.shape["var"]
    groups = mesh.shape["sec"] * var_size
    in_specs = (
        P(("sec", "var"), "trait"),
        P(("sec", "var"), None, None),
        P(("sec", "var"), None, None),
        P(),
        P(("sec", "var")),
        P(("sec", "var")),
    )
    return jax.shard_map(
        functools.partial(on_device, groups, var_size),
        mesh=mesh, in_specs=in_specs, out_specs=P(("sec", "var"), "trait"), check_vma=False,
    )
```

```python
import functools

import jax
import jax.numpy as jnp
from jax import lax
from jax.experimental import pallas as pl
from jax.experimental.pallas import tpu as pltpu
from jax.sharding import PartitionSpec as P

BLK = 128
WIN = 4
FIRST = 4
LAST = 8
FOREIGN_LATE = 1
LATE = LAST + FOREIGN_LATE * FIRST
CHUNK = 4
HEADS = ()
FIRST_AT = 5
AHEAD = 2
EAGER = 1
BY_PARTS = 3
SPLIT = 3
GROUP = 8
REDO = 8
DELAY = 1
MESH = pl.DeviceIdType.MESH


def cut(at, stop, sizes=()):
    sizes, out = list(sizes), []
    while at < stop:
        size = min(sizes.pop(0) if sizes else CHUNK, stop - at)
        out.append((at, size))
        at += size
    return out


def job_list(blocks):
    rows = blocks * BLK
    late = blocks - LAST
    begin = late - FIRST

    def own(kind, chunks):
        return [(kind, at, size, at * BLK, blocks + at) for at, size in chunks]

    def foreign(kind, at, size, side):
        land = side * LATE + at - (blocks - LATE) if FOREIGN_LATE else side * 2 * blocks + at
        return (kind, at, size, rows + (side * FIRST + at - begin) * BLK, land)

    first = cut(begin, late)
    main = own("own", cut(CHUNK, begin, HEADS) + cut(0, CHUNK) + cut(late, blocks))
    taken = [foreign(kind, at, size, side) for at, size in first for side, kind in enumerate(("left", "right"))]
    return main[:FIRST_AT] + own("first", first) + main[FIRST_AT:] + taken


def mixed_kernel(
    jobs, blocks, groups, var_size,
    z_ref, band_ref, mix_ref, ld_ref, start_ref, count_ref, ext_ref, ldv_ref, part_ref, starts, counts, touched,
    zb, bandv, w, gathered, mv, results, late_ref,
    z_sem, ld_sem, win_sem, band_sem, mix_sem, main_send, side_send, edge_recv, first_recv, in_recv, out_recv, halo_recv,
):
    t = lax.axis_index("trait")
    g = lax.axis_index("sec") * var_size + lax.axis_index("var")
    x_peer = t + 1 - 2 * lax.rem(t, 2)
    y_peer = t + 2 - 4 * (t // 2)
    far_peer = x_peer + y_peer - t
    peers = (t, x_peer, y_peer, far_peer)
    others = range(1, len(peers))
    right = {"sec": (g + 1) // var_size, "var": lax.rem(g + 1, var_size)}
    left_g = lax.rem(g + groups - 1, groups)
    left = {"sec": left_g // var_size, "var": lax.rem(left_g, var_size)}
    has_left, has_right = g > 0, g < groups - 1
    rows = blocks * BLK
    count_jobs = len(jobs)
    order = range(count_jobs)
    own_jobs = [c for c in order if jobs[c][0] == "own"]
    first_jobs = [c for c in order if jobs[c][0] == "first"]
    foreign = [c for c in order if jobs[c][0] in ("left", "right")]
    late = blocks - LAST
    begin = late - FIRST

    barrier = pltpu.get_barrier_semaphore()

    def greet(device):
        pl.semaphore_signal(barrier, inc=1, device_id=device, device_id_type=MESH)

    for j in others:
        greet({"trait": peers[j]})
    pl.when(has_left)(lambda: greet(left))
    pl.when(has_right)(lambda: greet(right))

    def remote(src, dst, send, recv, device):
        return pltpu.make_async_remote_copy(
            src_ref=src, dst_ref=dst, send_sem=send, recv_sem=recv,
            device_id=device, device_id_type=MESH,
        )

    def gated(c, act):
        kind = jobs[c][0]
        if kind == "left":
            pl.when(has_left)(act)
        elif kind == "right":
            pl.when(has_right)(act)
        else:
            act()

    own_first = first_jobs + own_jobs

    def load_band(k):
        group = [first_jobs, own_jobs[:1], own_jobs[1:]][k]
        for c in group:
            part = pl.ds(jobs[c][1], jobs[c][2])
            pltpu.make_async_copy(band_ref.at[part], bandv.at[part], band_sem.at[k]).start()
        return sum(jobs[c][2] for c in group)

    def wait_band(k, size):
        part = pl.ds(0, size)
        pltpu.make_async_copy(band_ref.at[part], bandv.at[part], band_sem.at[k]).wait()

    def load_rows(k, at, stop):
        part = pl.ds(at * BLK, (stop - at) * BLK)
        return pltpu.make_async_copy(z_ref.at[part], zb.at[pl.ds((at + 1) * BLK, (stop - at) * BLK)], z_sem.at[k])

    cuts = [0, CHUNK - 1, 2 * CHUNK + 1, begin - 1, late + 1, blocks]
    load_z = [load_rows(k, *span) for k, span in enumerate(zip(cuts[:-1], cuts[1:]))]
    load_z[3].start()
    band_sizes = [load_band(0)]
    load_z[1].start()
    band_sizes.append(load_band(1))

    load_mix = [
        pltpu.make_async_copy(
            mix_ref.at[
                pl.ds(pl.multiple_of(taken * BLK, BLK), BLK), pl.ds(pl.multiple_of(given * BLK, BLK), BLK)
            ],
            mv.at[pl.ds(i * BLK, BLK), pl.ds(j * BLK, BLK)],
            mix_sem,
        )
        for i, taken in enumerate(peers)
        for j, given in enumerate(peers)
    ]
    load_ld = pltpu.make_async_copy(ld_ref, ldv_ref, ld_sem)
    load_windows = [
        pltpu.make_async_copy(start_ref, starts, win_sem.at[0]),
        pltpu.make_async_copy(count_ref, counts, win_sem.at[1]),
    ]

    @pl.when(jnp.logical_not(has_left))
    def _():
        zb[pl.ds(0, BLK), :] = jnp.zeros((BLK, BLK), zb.dtype)

    @pl.when(jnp.logical_not(has_right))
    def _():
        zb[pl.ds(rows + BLK, BLK), :] = jnp.zeros((BLK, BLK), zb.dtype)

    edge_right = remote(
        z_ref.at[pl.ds(rows - BLK, BLK)], zb.at[pl.ds(0, BLK)], side_send.at[0], edge_recv.at[0], right
    )
    edge_left = remote(
        z_ref.at[pl.ds(0, BLK)], zb.at[pl.ds(rows + BLK, BLK)], side_send.at[1], edge_recv.at[1], left
    )

    def whiten(c):
        _, start, size, _, _ = jobs[c]
        k = 0 if c in first_jobs else 1 if c == own_jobs[0] else 2
        if band_sizes[k]:
            wait_band(k, band_sizes[k])
            band_sizes[k] = 0
        if start + size == blocks:
            pl.when(has_right)(edge_left.wait_recv)
        if start == 0:
            pl.when(has_left)(edge_right.wait_recv)

        def one(i, carry):
            b = start + i
            row = pl.multiple_of(b * BLK, BLK)
            sums = jnp.dot(bandv[b], zb[pl.ds(row, 3 * BLK), :], preferred_element_type=jnp.float32)
            w[pl.ds(row, BLK), :] = sums.astype(w.dtype)
            return carry

        lax.fori_loop(0, size, one, 0, unroll=True)

    def first(c):
        side = 0 if jobs[c][0] == "left" else 1
        at = pl.ds(jobs[c][1] * BLK, jobs[c][2] * BLK)
        return remote(
            w.at[at], w.at[pl.ds(jobs[c][3], jobs[c][2] * BLK)],
            side_send.at[side], first_recv.at[foreign.index(c)], (right, left)[side],
        ), (has_right, has_left)[side]

    def part_rows(c):
        return jobs[c][2] * BLK // len(peers)

    def part_of(c, peer):
        part = part_rows(c)
        return pl.ds(pl.multiple_of(jobs[c][3] + peer * part, part), part)

    def view(ref, at, c, peer):
        part = part_rows(c)
        if part == BLK:
            return ref.at[at + peer]
        row = peer * part
        return ref.at[at + row // BLK, pl.ds(pl.multiple_of(lax.rem(row, BLK), part), part)]

    def land_of(c, peer):
        return view(late_ref if FOREIGN_LATE and c in foreign else ext_ref, jobs[c][4], c, peer)

    def share_of(c):
        return pl.ds(jobs[c][3] // len(peers), part_rows(c))

    def send_sem(c):
        return {"left": side_send.at[1], "right": side_send.at[0]}.get(jobs[c][0], main_send)

    def sends_in(c):
        return [
            remote(
                w.at[part_of(c, peers[j])], gathered.at[j - 1, share_of(c)],
                send_sem(c), in_recv.at[c], {"trait": peers[j]},
            )
            for j in others
        ]

    def sends_out(c):
        return [
            remote(
                results.at[j - 1, share_of(c)], land_of(c, t),
                send_sem(c), out_sem(c, j), {"trait": peers[j]},
            )
            for j in others
        ]

    def out_sem(c, j):
        return out_recv.at[count_jobs + 2 * c + j - 2 if c in own_jobs[:SPLIT] and j > 1 else c]

    def await_part(c, j):
        ref = results.at[j - 1, share_of(c)]
        remote(ref, ref, send_sem(c), out_sem(c, j), {"trait": x_peer}).wait_recv()

    def await_in(c):
        ref = gathered.at[:, share_of(c)]
        remote(ref, ref, send_sem(c), in_recv.at[c], {"trait": x_peer}).wait_recv()

    def await_out(c):
        ref = results.at[:, share_of(c)]
        remote(ref, ref, send_sem(c), out_recv.at[c], {"trait": x_peer}).wait_recv()

    def start_in(c):
        def act():
            if c in foreign:
                first(c)[0].wait_recv()
            for copy in sends_in(c):
                copy.start()

        gated(c, act)

    def mix(c):
        def act():
            await_in(c)
            all_traits = jnp.concatenate(
                [w[part_of(c, t), :]] + [gathered[j - 1, share_of(c), :] for j in others], axis=1
            )
            sums = jnp.dot(all_traits, mv[...], preferred_element_type=jnp.float32).astype(w.dtype)
            land_of(c, t)[...] = sums[:, :BLK]
            for j in others:
                results[j - 1, share_of(c), :] = sums[:, j * BLK : (j + 1) * BLK]
            for copy in sends_out(c):
                copy.start()

        gated(c, act)

    by_parts = own_jobs[:BY_PARTS]

    def is_late(c):
        return jobs[c][1] >= late

    def halo_at(c, side):
        start = jobs[c][1]
        if is_late(c):
            return late_ref, side * LATE + start - (blocks - LATE)
        return ext_ref, side * 2 * blocks + start

    def send_halo(c, side, part):
        ref, at = halo_at(c, side)
        if part is None:
            source, target = ext_ref.at[pl.ds(jobs[c][4], jobs[c][2])], ref.at[pl.ds(at, jobs[c][2])]
        else:
            source, target = view(ext_ref, jobs[c][4], c, part), view(ref, at, c, part)
        copy = remote(
            source, target, side_send.at[side], halo_recv.at[side, int(is_late(c))], right if side == 0 else left
        )
        return copy

    at_end = has_left & (g == var_size - 1)
    held = []

    def send_halos(c, which):
        parts = [None if j is None else peers[j] for j in which]
        for part in parts:
            pl.when(has_right)(send_halo(c, 0, part).start)
            pl.when(has_left & jnp.logical_not(at_end))(send_halo(c, 1, part).start)
        if held and held[-1][0] == c:
            held[-1][1].extend(send_halo(c, 1, part) for part in parts)
        else:
            held.append((c, [send_halo(c, 1, part) for part in parts]))
        release(DELAY)

    def release(keep):
        while len(held) > keep:
            copies = held.pop(0)[1]

            @pl.when(at_end)
            def _():
                for copy in copies:
                    copy.start()

    load_z[3].wait()
    pending = list(own_first)

    def whiten_upto(i):
        if i < count_jobs and i in pending:
            pending.remove(i)
            whiten(i)

    for c in first_jobs:
        whiten_upto(c)
    for k in (2, 0, 4):
        load_z[k].start()
    band_sizes.append(load_band(2))
    load_z[1].wait()
    for c in range(EAGER):
        whiten_upto(c)
    pl.semaphore_wait(barrier, len(others) + has_left.astype(jnp.int32) + has_right.astype(jnp.int32))
    for c in foreign:
        copy, sends = first(c)
        pl.when(sends)(copy.start)
    for c in range(EAGER):
        start_in(c)
    pl.when(has_right)(edge_right.start)
    pl.when(has_left)(edge_left.start)
    for copy in load_mix:
        copy.start()
    for k in (2, 0, 4):
        load_z[k].wait()
    for c in range(EAGER, AHEAD):
        whiten_upto(c)
    for c in range(EAGER, AHEAD):
        start_in(c)
    load_ld.start()
    for copy in load_windows:
        copy.start()
    whiten_upto(AHEAD)
    for b in (*range(blocks - LATE, blocks), *range(3 * blocks - LATE, 3 * blocks + 1)):
        ext_ref[b] = jnp.zeros((BLK, BLK), ext_ref.dtype)
    pltpu.make_async_copy(mix_ref, mv, mix_sem).wait()
    for copy in load_windows:
        copy.wait()
    for i in range(part_ref.shape[0] // REDO):
        found = 0
        for u in range(i * REDO, (i + 1) * REDO):
            at = starts[u] - (g - 1) * blocks
            stop = at + counts[u]
            in_left = jnp.clip(blocks - at, 0, 1) * jnp.clip(stop - (blocks - LATE), 0, 1)
            in_right = jnp.clip(stop - (3 * blocks - LATE), 0, 1)
            found = found + in_left + in_right
        touched[i] = found

    def settle(c):
        if c in own_jobs[:SPLIT]:
            for j in others:
                await_part(c, j)
                send_halos(c, (j,))
            return
        gated(c, lambda: await_out(c))
        if c in own_jobs:
            send_halos(c, others if c in by_parts else (None,))

    for i in range(count_jobs + 1):
        if i < count_jobs:
            mix(i)
            if i in by_parts:
                send_halos(i, (0,))
        if i + AHEAD < count_jobs:
            start_in(i + AHEAD)
        if i >= 1 and i - 1 not in foreign:
            settle(i - 1)
        whiten_upto(i + AHEAD + 1)

    release(0)

    def wait_halos(last):
        size = sum(jobs[c][2] for c in own_jobs if is_late(c) == last)
        ref = late_ref.at[pl.ds(0, size)] if last else ext_ref.at[pl.ds(0, size)]
        from_right = remote(ref, ref, side_send.at[1], halo_recv.at[1, int(last)], right)
        from_left = remote(ref, ref, side_send.at[0], halo_recv.at[0, int(last)], left)
        pl.when(has_right)(from_right.wait_recv)
        pl.when(has_left)(from_left.wait_recv)

    if not FOREIGN_LATE:
        for c in foreign:
            settle(c)
    load_ld.wait()
    wait_halos(False)

    nothing = 3 * blocks

    def early(i, carry):
        for k in range(GROUP):
            u = i * GROUP + k
            at = starts[u] - (g - 1) * blocks
            many = counts[u]
            parts = []
            for s in range(WIN):
                b = jnp.clip(at + s, 0, nothing)
                if s:
                    b = nothing + (b - nothing) * jnp.clip(many - s, 0, 1)
                parts.append(ext_ref[b])
            sums = jnp.dot(ldv_ref[u], jnp.concatenate(parts, axis=0), preferred_element_type=jnp.float32)
            part_ref[u] = sums.astype(part_ref.dtype)
        return carry

    lax.fori_loop(0, part_ref.shape[0] // GROUP, early, 0)

    if FOREIGN_LATE:
        for c in foreign:
            settle(c)

    def sent(size, sem):
        ref = ext_ref.at[pl.ds(0, size)]
        return remote(ref, ref, sem, edge_recv.at[0], right)

    sent(6 * blocks // len(peers), main_send).wait_send()
    side_size = blocks + 1 + 6 * FIRST // len(peers)
    pl.when(has_right)(sent(side_size, side_send.at[0]).wait_send)
    pl.when(has_left)(sent(side_size, side_send.at[1]).wait_send)
    wait_halos(True)
    for side in (0, 1):
        for k in range(LATE):
            ext_ref[(2 * side + 1) * blocks - LATE + k] = late_ref[side * LATE + k]


def mixed_with_neighbours(z_typed, band_inverse, trait_mix, ld_untyped, win_start, win_count, groups, var_size):
    rows = z_typed.shape[0]
    blocks = rows // BLK
    jobs = job_list(blocks)
    peers = trait_mix.shape[0] // BLK
    untyped = ld_untyped.shape[0]
    work = rows + 2 * FIRST * BLK
    count = len(jobs)
    taken = sum(job[0] in ("left", "right") for job in jobs)
    dma = pltpu.SemaphoreType.DMA
    kind = z_typed.dtype
    hbm = pl.BlockSpec(memory_space=pl.ANY)
    vmem = pl.BlockSpec(memory_space=pltpu.VMEM)
    smem = pl.BlockSpec(memory_space=pltpu.SMEM)
    return pl.pallas_call(
        functools.partial(mixed_kernel, jobs, blocks, groups, var_size),
        out_shape=(
            pltpu.VMEM((3 * blocks + 1, BLK, BLK), kind),
            pltpu.VMEM(ld_untyped.shape, kind),
            pltpu.VMEM((untyped, BLK, BLK), kind),
            pltpu.SMEM(win_start.shape, win_start.dtype),
            pltpu.SMEM(win_count.shape, win_count.dtype),
            pltpu.SMEM((untyped // REDO,), win_count.dtype),
        ),
        in_specs=[hbm] * 6,
        out_specs=(vmem, vmem, vmem, smem, smem, smem),
        scratch_shapes=[
            pltpu.VMEM((rows + 2 * BLK, BLK), kind),
            pltpu.VMEM(band_inverse.shape, kind),
            pltpu.VMEM((work, BLK), kind),
            pltpu.VMEM((peers - 1, work // peers, BLK), kind),
            pltpu.VMEM(trait_mix.shape, kind),
            pltpu.VMEM((peers - 1, work // peers, BLK), kind),
            pltpu.VMEM((2 * LATE, BLK, BLK), kind),
            dma((5,)), dma, dma((2,)), dma((3,)), dma, dma, dma((2,)), dma((2,)), dma((taken,)),
            dma((count,)), dma((count + 2 * SPLIT,)), dma((2, 2)),
        ],
        compiler_params=pltpu.CompilerParams(
            collective_id=0, has_side_effects=True, vmem_limit_bytes=32 * 1024 * 1024
        ),
        name="mixed_kernel",
    )(*(
        pltpu.with_memory_space_constraint(v, pltpu.HBM)
        for v in (z_typed, band_inverse, trait_mix, ld_untyped, win_start, win_count)
    ))


def impute_kernel(blocks, var_size, start_ref, count_ref, touched, ext_ref, ld_ref, part_ref, out_ref, fixed, sem):
    g = lax.axis_index("sec") * var_size + lax.axis_index("var")
    nothing = 3 * blocks

    def send(ref, i):
        part = pl.ds(i * REDO, REDO)
        pltpu.make_async_copy(ref.at[part], out_ref.at[part], sem).start()

    def redo(i):
        for u in range(i * REDO, (i + 1) * REDO):
            at = start_ref[u] - (g - 1) * blocks
            many = count_ref[u]
            parts = []
            for s in range(WIN):
                b = jnp.clip(at + s, 0, nothing)
                parts.append(ext_ref[jnp.where(s < many, b, nothing) if s else b])
            sums = jnp.dot(ld_ref[u], jnp.concatenate(parts, axis=0), preferred_element_type=jnp.float32)
            fixed[u] = sums.astype(fixed.dtype)
        send(fixed, i)

    for i in range(part_ref.shape[0] // REDO):
        pl.when(touched[i] == 0)(functools.partial(send, part_ref, i))
    for i in range(part_ref.shape[0] // REDO):
        pl.when(touched[i] != 0)(functools.partial(redo, i))
    pltpu.make_async_copy(part_ref, out_ref, sem).wait()


def impute(ext, ld_untyped, part, starts, counts, touched, var_size):
    untyped = ld_untyped.shape[0]
    blocks = ext.shape[0] // 3
    cols = ext.shape[2]
    vmem = pl.BlockSpec(memory_space=pltpu.VMEM)
    smem = pl.BlockSpec(memory_space=pltpu.SMEM)
    return pl.pallas_call(
        functools.partial(impute_kernel, blocks, var_size),
        in_specs=[smem, smem, smem, vmem, vmem, vmem],
        out_specs=pl.BlockSpec(memory_space=pl.ANY),
        scratch_shapes=[pltpu.VMEM((untyped, BLK, cols), ext.dtype), pltpu.SemaphoreType.DMA],
        out_shape=jax.ShapeDtypeStruct((untyped, BLK, cols), ext.dtype),
        compiler_params=pltpu.CompilerParams(vmem_limit_bytes=24 * 1024 * 1024),
        name="impute_kernel",
    )(starts, counts, touched, ext, ld_untyped, part)


def on_device(groups, var_size, z_typed, band_inverse, ld_untyped, trait_mix, win_start, win_count):
    ext, ld_near, part, starts, counts, touched = mixed_with_neighbours(
        z_typed, band_inverse, trait_mix, ld_untyped, win_start, win_count, groups, var_size
    )
    imputed = impute(ext, ld_near, part, starts, counts, touched, var_size)
    return imputed.reshape(ld_untyped.shape[0] * BLK, z_typed.shape[1])


def solution(mesh):
    var_size = mesh.shape["var"]
    groups = mesh.shape["sec"] * var_size
    in_specs = (
        P(("sec", "var"), "trait"),
        P(("sec", "var"), None, None),
        P(("sec", "var"), None, None),
        P(),
        P(("sec", "var")),
        P(("sec", "var")),
    )
    return jax.shard_map(
        functools.partial(on_device, groups, var_size),
        mesh=mesh, in_specs=in_specs, out_specs=P(("sec", "var"), "trait"), check_vma=False,
    )
```

```python
import functools

import jax
import jax.numpy as jnp
from jax import lax
from jax.experimental import pallas as pl
from jax.experimental.pallas import tpu as pltpu
from jax.sharding import PartitionSpec as P

BLK = 128
WIN = 4
FIRST = 4
LAST = 8
FOREIGN_LATE = 1
LATE = LAST + FOREIGN_LATE * FIRST
CHUNK = 4
HEADS = ()
FIRST_AT = 5
AHEAD = 2
EAGER = 1
BY_PARTS = 3
SPLIT = 3
GROUP = 8
REDO = 8
DELAY = 1
MESH = pl.DeviceIdType.MESH


def cut(at, stop, sizes=()):
    sizes, out = list(sizes), []
    while at < stop:
        size = min(sizes.pop(0) if sizes else CHUNK, stop - at)
        out.append((at, size))
        at += size
    return out


def job_list(blocks):
    rows = blocks * BLK
    late = blocks - LAST
    begin = late - FIRST

    def own(kind, chunks):
        return [(kind, at, size, at * BLK, blocks + at) for at, size in chunks]

    def foreign(kind, at, size, side):
        land = side * LATE + at - (blocks - LATE) if FOREIGN_LATE else side * 2 * blocks + at
        return (kind, at, size, rows + (side * FIRST + at - begin) * BLK, land)

    first = cut(begin, late)
    main = own("own", cut(CHUNK, begin, HEADS) + cut(0, CHUNK) + cut(late, blocks))
    taken = [foreign(kind, at, size, side) for at, size in first for side, kind in enumerate(("left", "right"))]
    return main[:FIRST_AT] + own("first", first) + main[FIRST_AT:] + taken


def mixed_kernel(
    jobs, blocks, groups, var_size,
    z_ref, band_ref, mix_ref, ld_ref, start_ref, count_ref, ext_ref, ldv_ref, part_ref, starts, counts, touched,
    zb, bandv, w, gathered, mv, results, late_ref,
    z_sem, ld_sem, win_sem, band_sem, mix_sem, main_send, side_send, edge_recv, first_recv, in_recv, out_recv, halo_recv,
):
    t = lax.axis_index("trait")
    g = lax.axis_index("sec") * var_size + lax.axis_index("var")
    x_peer = t + 1 - 2 * lax.rem(t, 2)
    y_peer = t + 2 - 4 * (t // 2)
    far_peer = x_peer + y_peer - t
    peers = (t, x_peer, y_peer, far_peer)
    others = range(1, len(peers))
    right = {"sec": (g + 1) // var_size, "var": lax.rem(g + 1, var_size)}
    left_g = lax.rem(g + groups - 1, groups)
    left = {"sec": left_g // var_size, "var": lax.rem(left_g, var_size)}
    has_left, has_right = g > 0, g < groups - 1
    rows = blocks * BLK
    count_jobs = len(jobs)
    order = range(count_jobs)
    own_jobs = [c for c in order if jobs[c][0] == "own"]
    first_jobs = [c for c in order if jobs[c][0] == "first"]
    foreign = [c for c in order if jobs[c][0] in ("left", "right")]
    late = blocks - LAST
    begin = late - FIRST

    barrier = pltpu.get_barrier_semaphore()

    def greet(device):
        pl.semaphore_signal(barrier, inc=1, device_id=device, device_id_type=MESH)

    for j in others:
        greet({"trait": peers[j]})
    pl.when(has_left)(lambda: greet(left))
    pl.when(has_right)(lambda: greet(right))

    def remote(src, dst, send, recv, device):
        return pltpu.make_async_remote_copy(
            src_ref=src, dst_ref=dst, send_sem=send, recv_sem=recv,
            device_id=device, device_id_type=MESH,
        )

    def gated(c, act):
        kind = jobs[c][0]
        if kind == "left":
            pl.when(has_left)(act)
        elif kind == "right":
            pl.when(has_right)(act)
        else:
            act()

    own_first = first_jobs + own_jobs

    def load_band(k):
        group = [first_jobs, own_jobs[:1], own_jobs[1:]][k]
        for c in group:
            part = pl.ds(jobs[c][1], jobs[c][2])
            pltpu.make_async_copy(band_ref.at[part], bandv.at[part], band_sem.at[k]).start()
        return sum(jobs[c][2] for c in group)

    def wait_band(k, size):
        part = pl.ds(0, size)
        pltpu.make_async_copy(band_ref.at[part], bandv.at[part], band_sem.at[k]).wait()

    def load_rows(k, at, stop):
        part = pl.ds(at * BLK, (stop - at) * BLK)
        return pltpu.make_async_copy(z_ref.at[part], zb.at[pl.ds((at + 1) * BLK, (stop - at) * BLK)], z_sem.at[k])

    cuts = [0, CHUNK - 1, 2 * CHUNK + 1, begin - 1, late + 1, blocks]
    load_z = [load_rows(k, *span) for k, span in enumerate(zip(cuts[:-1], cuts[1:]))]
    load_z[3].start()
    band_sizes = [load_band(0)]
    load_z[1].start()
    band_sizes.append(load_band(1))

    load_mix = [
        pltpu.make_async_copy(
            mix_ref.at[
                pl.ds(pl.multiple_of(taken * BLK, BLK), BLK), pl.ds(pl.multiple_of(given * BLK, BLK), BLK)
            ],
            mv.at[pl.ds(i * BLK, BLK), pl.ds(j * BLK, BLK)],
            mix_sem,
        )
        for i, taken in enumerate(peers)
        for j, given in enumerate(peers)
    ]
    load_ld = pltpu.make_async_copy(ld_ref, ldv_ref, ld_sem)
    load_windows = [
        pltpu.make_async_copy(start_ref, starts, win_sem.at[0]),
        pltpu.make_async_copy(count_ref, counts, win_sem.at[1]),
    ]

    @pl.when(jnp.logical_not(has_left))
    def _():
        zb[pl.ds(0, BLK), :] = jnp.zeros((BLK, BLK), zb.dtype)

    @pl.when(jnp.logical_not(has_right))
    def _():
        zb[pl.ds(rows + BLK, BLK), :] = jnp.zeros((BLK, BLK), zb.dtype)

    edge_right = remote(
        z_ref.at[pl.ds(rows - BLK, BLK)], zb.at[pl.ds(0, BLK)], side_send.at[0], edge_recv.at[0], right
    )
    edge_left = remote(
        z_ref.at[pl.ds(0, BLK)], zb.at[pl.ds(rows + BLK, BLK)], side_send.at[1], edge_recv.at[1], left
    )

    def whiten(c):
        _, start, size, _, _ = jobs[c]
        k = 0 if c in first_jobs else 1 if c == own_jobs[0] else 2
        if band_sizes[k]:
            wait_band(k, band_sizes[k])
            band_sizes[k] = 0
        if start + size == blocks:
            pl.when(has_right)(edge_left.wait_recv)
        if start == 0:
            pl.when(has_left)(edge_right.wait_recv)

        def one(i, carry):
            b = start + i
            row = pl.multiple_of(b * BLK, BLK)
            sums = jnp.dot(bandv[b], zb[pl.ds(row, 3 * BLK), :], preferred_element_type=jnp.float32)
            w[pl.ds(row, BLK), :] = sums.astype(w.dtype)
            return carry

        lax.fori_loop(0, size, one, 0, unroll=True)

    def first(c):
        side = 0 if jobs[c][0] == "left" else 1
        at = pl.ds(jobs[c][1] * BLK, jobs[c][2] * BLK)
        return remote(
            w.at[at], w.at[pl.ds(jobs[c][3], jobs[c][2] * BLK)],
            side_send.at[side], first_recv.at[foreign.index(c)], (right, left)[side],
        ), (has_right, has_left)[side]

    def part_rows(c):
        return jobs[c][2] * BLK // len(peers)

    def part_of(c, peer):
        part = part_rows(c)
        return pl.ds(pl.multiple_of(jobs[c][3] + peer * part, part), part)

    def view(ref, at, c, peer):
        part = part_rows(c)
        if part == BLK:
            return ref.at[at + peer]
        row = peer * part
        return ref.at[at + row // BLK, pl.ds(pl.multiple_of(lax.rem(row, BLK), part), part)]

    def land_of(c, peer):
        return view(late_ref if FOREIGN_LATE and c in foreign else ext_ref, jobs[c][4], c, peer)

    def share_of(c):
        return pl.ds(jobs[c][3] // len(peers), part_rows(c))

    def send_sem(c):
        return {"left": side_send.at[1], "right": side_send.at[0]}.get(jobs[c][0], main_send)

    def sends_in(c):
        return [
            remote(
                w.at[part_of(c, peers[j])], gathered.at[j - 1, share_of(c)],
                send_sem(c), in_recv.at[c], {"trait": peers[j]},
            )
            for j in others
        ]

    def sends_out(c):
        return [
            remote(
                results.at[j - 1, share_of(c)], land_of(c, t),
                send_sem(c), out_sem(c, j), {"trait": peers[j]},
            )
            for j in others
        ]

    def out_sem(c, j):
        return out_recv.at[count_jobs + 2 * c + j - 2 if c in own_jobs[:SPLIT] and j > 1 else c]

    def await_part(c, j):
        ref = results.at[j - 1, share_of(c)]
        remote(ref, ref, send_sem(c), out_sem(c, j), {"trait": x_peer}).wait_recv()

    def await_in(c):
        ref = gathered.at[:, share_of(c)]
        remote(ref, ref, send_sem(c), in_recv.at[c], {"trait": x_peer}).wait_recv()

    def await_out(c):
        ref = results.at[:, share_of(c)]
        remote(ref, ref, send_sem(c), out_recv.at[c], {"trait": x_peer}).wait_recv()

    def start_in(c):
        def act():
            if c in foreign:
                first(c)[0].wait_recv()
            for copy in sends_in(c):
                copy.start()

        gated(c, act)

    def mix(c):
        def act():
            await_in(c)
            all_traits = jnp.concatenate(
                [w[part_of(c, t), :]] + [gathered[j - 1, share_of(c), :] for j in others], axis=1
            )
            sums = jnp.dot(all_traits, mv[...], preferred_element_type=jnp.float32).astype(w.dtype)
            land_of(c, t)[...] = sums[:, :BLK]
            for j in others:
                results[j - 1, share_of(c), :] = sums[:, j * BLK : (j + 1) * BLK]
            for copy in sends_out(c):
                copy.start()

        gated(c, act)

    by_parts = own_jobs[:BY_PARTS]

    def is_late(c):
        return jobs[c][1] >= late

    def halo_at(c, side):
        start = jobs[c][1]
        if is_late(c):
            return late_ref, side * LATE + start - (blocks - LATE)
        return ext_ref, side * 2 * blocks + start

    def send_halo(c, side, part):
        ref, at = halo_at(c, side)
        if part is None:
            source, target = ext_ref.at[pl.ds(jobs[c][4], jobs[c][2])], ref.at[pl.ds(at, jobs[c][2])]
        else:
            source, target = view(ext_ref, jobs[c][4], c, part), view(ref, at, c, part)
        copy = remote(
            source, target, side_send.at[side], halo_recv.at[side, int(is_late(c))], right if side == 0 else left
        )
        return copy

    at_end = has_left & ((g == var_size - 1) | (g == var_size + 1))
    held = []

    def send_halos(c, which):
        parts = [None if j is None else peers[j] for j in which]
        for part in parts:
            pl.when(has_right)(send_halo(c, 0, part).start)
            pl.when(has_left & jnp.logical_not(at_end))(send_halo(c, 1, part).start)
        if held and held[-1][0] == c:
            held[-1][1].extend(send_halo(c, 1, part) for part in parts)
        else:
            held.append((c, [send_halo(c, 1, part) for part in parts]))
        release(DELAY)

    def release(keep):
        while len(held) > keep:
            copies = held.pop(0)[1]

            @pl.when(at_end)
            def _():
                for copy in copies:
                    copy.start()

    load_z[3].wait()
    pending = list(own_first)

    def whiten_upto(i):
        if i < count_jobs and i in pending:
            pending.remove(i)
            whiten(i)

    for c in first_jobs:
        whiten_upto(c)
    for k in (2, 0, 4):
        load_z[k].start()
    band_sizes.append(load_band(2))
    load_z[1].wait()
    for c in range(EAGER):
        whiten_upto(c)
    pl.semaphore_wait(barrier, len(others) + has_left.astype(jnp.int32) + has_right.astype(jnp.int32))
    for c in foreign:
        copy, sends = first(c)
        pl.when(sends)(copy.start)
    for c in range(EAGER):
        start_in(c)
    pl.when(has_right)(edge_right.start)
    pl.when(has_left)(edge_left.start)
    for copy in load_mix:
        copy.start()
    for k in (2, 0, 4):
        load_z[k].wait()
    for c in range(EAGER, AHEAD):
        whiten_upto(c)
    for c in range(EAGER, AHEAD):
        start_in(c)
    load_ld.start()
    for copy in load_windows:
        copy.start()
    whiten_upto(AHEAD)
    for b in (*range(blocks - LATE, blocks), *range(3 * blocks - LATE, 3 * blocks + 1)):
        ext_ref[b] = jnp.zeros((BLK, BLK), ext_ref.dtype)
    pltpu.make_async_copy(mix_ref, mv, mix_sem).wait()
    for copy in load_windows:
        copy.wait()
    for i in range(part_ref.shape[0] // REDO):
        found = 0
        for u in range(i * REDO, (i + 1) * REDO):
            at = starts[u] - (g - 1) * blocks
            stop = at + counts[u]
            in_left = jnp.clip(blocks - at, 0, 1) * jnp.clip(stop - (blocks - LATE), 0, 1)
            in_right = jnp.clip(stop - (3 * blocks - LATE), 0, 1)
            found = found + in_left + in_right
        touched[i] = found

    def settle(c):
        if c in own_jobs[:SPLIT]:
            for j in others:
                await_part(c, j)
                send_halos(c, (j,))
            return
        gated(c, lambda: await_out(c))
        if c in own_jobs:
            send_halos(c, others if c in by_parts else (None,))

    for i in range(count_jobs + 1):
        if i < count_jobs:
            mix(i)
            if i in by_parts:
                send_halos(i, (0,))
        if i + AHEAD < count_jobs:
            start_in(i + AHEAD)
        if i >= 1 and i - 1 not in foreign:
            settle(i - 1)
        whiten_upto(i + AHEAD + 1)

    release(0)

    def wait_halos(last):
        size = sum(jobs[c][2] for c in own_jobs if is_late(c) == last)
        ref = late_ref.at[pl.ds(0, size)] if last else ext_ref.at[pl.ds(0, size)]
        from_right = remote(ref, ref, side_send.at[1], halo_recv.at[1, int(last)], right)
        from_left = remote(ref, ref, side_send.at[0], halo_recv.at[0, int(last)], left)
        pl.when(has_right)(from_right.wait_recv)
        pl.when(has_left)(from_left.wait_recv)

    if not FOREIGN_LATE:
        for c in foreign:
            settle(c)
    load_ld.wait()
    wait_halos(False)

    nothing = 3 * blocks

    def early(i, carry):
        for k in range(GROUP):
            u = i * GROUP + k
            at = starts[u] - (g - 1) * blocks
            many = counts[u]
            parts = []
            for s in range(WIN):
                b = jnp.clip(at + s, 0, nothing)
                if s:
                    b = nothing + (b - nothing) * jnp.clip(many - s, 0, 1)
                parts.append(ext_ref[b])
            sums = jnp.dot(ldv_ref[u], jnp.concatenate(parts, axis=0), preferred_element_type=jnp.float32)
            part_ref[u] = sums.astype(part_ref.dtype)
        return carry

    lax.fori_loop(0, part_ref.shape[0] // GROUP, early, 0)

    if FOREIGN_LATE:
        for c in foreign:
            settle(c)

    def sent(size, sem):
        ref = ext_ref.at[pl.ds(0, size)]
        return remote(ref, ref, sem, edge_recv.at[0], right)

    sent(6 * blocks // len(peers), main_send).wait_send()
    side_size = blocks + 1 + 6 * FIRST // len(peers)
    pl.when(has_right)(sent(side_size, side_send.at[0]).wait_send)
    pl.when(has_left)(sent(side_size, side_send.at[1]).wait_send)
    wait_halos(True)
    for side in (0, 1):
        for k in range(LATE):
            ext_ref[(2 * side + 1) * blocks - LATE + k] = late_ref[side * LATE + k]


def mixed_with_neighbours(z_typed, band_inverse, trait_mix, ld_untyped, win_start, win_count, groups, var_size):
    rows = z_typed.shape[0]
    blocks = rows // BLK
    jobs = job_list(blocks)
    peers = trait_mix.shape[0] // BLK
    untyped = ld_untyped.shape[0]
    work = rows + 2 * FIRST * BLK
    count = len(jobs)
    taken = sum(job[0] in ("left", "right") for job in jobs)
    dma = pltpu.SemaphoreType.DMA
    kind = z_typed.dtype
    hbm = pl.BlockSpec(memory_space=pl.ANY)
    vmem = pl.BlockSpec(memory_space=pltpu.VMEM)
    smem = pl.BlockSpec(memory_space=pltpu.SMEM)
    return pl.pallas_call(
        functools.partial(mixed_kernel, jobs, blocks, groups, var_size),
        out_shape=(
            pltpu.VMEM((3 * blocks + 1, BLK, BLK), kind),
            pltpu.VMEM(ld_untyped.shape, kind),
            pltpu.VMEM((untyped, BLK, BLK), kind),
            pltpu.SMEM(win_start.shape, win_start.dtype),
            pltpu.SMEM(win_count.shape, win_count.dtype),
            pltpu.SMEM((untyped // REDO,), win_count.dtype),
        ),
        in_specs=[hbm] * 6,
        out_specs=(vmem, vmem, vmem, smem, smem, smem),
        scratch_shapes=[
            pltpu.VMEM((rows + 2 * BLK, BLK), kind),
            pltpu.VMEM(band_inverse.shape, kind),
            pltpu.VMEM((work, BLK), kind),
            pltpu.VMEM((peers - 1, work // peers, BLK), kind),
            pltpu.VMEM(trait_mix.shape, kind),
            pltpu.VMEM((peers - 1, work // peers, BLK), kind),
            pltpu.VMEM((2 * LATE, BLK, BLK), kind),
            dma((5,)), dma, dma((2,)), dma((3,)), dma, dma, dma((2,)), dma((2,)), dma((taken,)),
            dma((count,)), dma((count + 2 * SPLIT,)), dma((2, 2)),
        ],
        compiler_params=pltpu.CompilerParams(
            collective_id=0, has_side_effects=True, vmem_limit_bytes=32 * 1024 * 1024
        ),
        name="mixed_kernel",
    )(*(
        pltpu.with_memory_space_constraint(v, pltpu.HBM)
        for v in (z_typed, band_inverse, trait_mix, ld_untyped, win_start, win_count)
    ))


def impute_kernel(blocks, var_size, start_ref, count_ref, touched, ext_ref, ld_ref, part_ref, out_ref, fixed, sem):
    g = lax.axis_index("sec") * var_size + lax.axis_index("var")
    nothing = 3 * blocks

    def send(ref, i):
        part = pl.ds(i * REDO, REDO)
        pltpu.make_async_copy(ref.at[part], out_ref.at[part], sem).start()

    def redo(i):
        for u in range(i * REDO, (i + 1) * REDO):
            at = start_ref[u] - (g - 1) * blocks
            many = count_ref[u]
            parts = []
            for s in range(WIN):
                b = jnp.clip(at + s, 0, nothing)
                parts.append(ext_ref[jnp.where(s < many, b, nothing) if s else b])
            sums = jnp.dot(ld_ref[u], jnp.concatenate(parts, axis=0), preferred_element_type=jnp.float32)
            fixed[u] = sums.astype(fixed.dtype)
        send(fixed, i)

    for i in range(part_ref.shape[0] // REDO):
        pl.when(touched[i] == 0)(functools.partial(send, part_ref, i))
    for i in range(part_ref.shape[0] // REDO):
        pl.when(touched[i] != 0)(functools.partial(redo, i))
    pltpu.make_async_copy(part_ref, out_ref, sem).wait()


def impute(ext, ld_untyped, part, starts, counts, touched, var_size):
    untyped = ld_untyped.shape[0]
    blocks = ext.shape[0] // 3
    cols = ext.shape[2]
    vmem = pl.BlockSpec(memory_space=pltpu.VMEM)
    smem = pl.BlockSpec(memory_space=pltpu.SMEM)
    return pl.pallas_call(
        functools.partial(impute_kernel, blocks, var_size),
        in_specs=[smem, smem, smem, vmem, vmem, vmem],
        out_specs=pl.BlockSpec(memory_space=pl.ANY),
        scratch_shapes=[pltpu.VMEM((untyped, BLK, cols), ext.dtype), pltpu.SemaphoreType.DMA],
        out_shape=jax.ShapeDtypeStruct((untyped, BLK, cols), ext.dtype),
        compiler_params=pltpu.CompilerParams(vmem_limit_bytes=24 * 1024 * 1024),
        name="impute_kernel",
    )(starts, counts, touched, ext, ld_untyped, part)


def on_device(groups, var_size, z_typed, band_inverse, ld_untyped, trait_mix, win_start, win_count):
    ext, ld_near, part, starts, counts, touched = mixed_with_neighbours(
        z_typed, band_inverse, trait_mix, ld_untyped, win_start, win_count, groups, var_size
    )
    imputed = impute(ext, ld_near, part, starts, counts, touched, var_size)
    return imputed.reshape(ld_untyped.shape[0] * BLK, z_typed.shape[1])


def solution(mesh):
    var_size = mesh.shape["var"]
    groups = mesh.shape["sec"] * var_size
    in_specs = (
        P(("sec", "var"), "trait"),
        P(("sec", "var"), None, None),
        P(("sec", "var"), None, None),
        P(),
        P(("sec", "var")),
        P(("sec", "var")),
    )
    return jax.shard_map(
        functools.partial(on_device, groups, var_size),
        mesh=mesh, in_specs=in_specs, out_specs=P(("sec", "var"), "trait"), check_vma=False,
    )
```
